32 devices in a mesh: rows: 4 (over y, x), pairs: 8 (over z, core).
Axes of the slice: x: 2, y: 2, z: 4, core: 2. Of those that a mesh axis runs over, the one named last changes fastest.
Arguments:
- latent: bfloat16 [8192, 3072], P('rows', 'pairs'), as said below
Outputs:
- rotated_latent: bfloat16 [8192, 3072], P('rows', 'pairs')
Inputs may be any that keep to these rules, and one draw needn't show every extreme that they name: `latent`: finite real entries.
All inputs are finite; a program needn't handle non-finite values.
Results may differ from the reference program's by a relative error of at most 0.0065.
Values may be sent and summed in bfloat16 or wider, within the bound.
No kernel may reach another device: no remote copies, remote signals or barrier semaphores. Data moves between devices by JAX's collectives and lax.ppermute only.
A program may use at most 64 MiB of HBM per device.

```python
import math
import jax
import jax.numpy as jnp
from jax import lax

BLK = 192
ROUNDS = 2
NS_ITERS = 2
NPOS = 8
ROWS = 8192
COLS = 3072


def draw_latent(key, part):
    k_base = jax.random.fold_in(key, 11)
    k_row = jax.random.fold_in(key, 12)
    k_col = jax.random.fold_in(key, 13)
    base = jax.random.normal(k_base, (ROWS, COLS), jnp.float32)
    place = jnp.arange(ROWS, dtype=jnp.float32)[:, None] / ROWS
    rough = jnp.exp(jax.random.uniform(k_row, (ROWS, 1), jnp.float32, -0.3, 0.3))
    row_scale = (1.0 + 2.0 * place) * rough
    col_scale = jnp.exp(jax.random.uniform(k_col, (1, COLS), jnp.float32, -0.3, 0.3))
    values = base * row_scale * col_scale
    return values.astype(jnp.bfloat16)


def setup_inputs(seed: int = 0) -> dict:
    streams_of = jax.random.split(jax.random.key(seed), 2)
    return {
        "latent": draw_latent(jax.random.fold_in(streams_of[1], 71), 0),
    }


def orthogonal(norms, cross):
    half = cross.shape[0]
    corr = cross / jnp.sqrt(norms[:half, None] * norms[None, half:])
    total = jnp.sqrt(2.0 * jnp.sum(corr * corr) + 1e-12)
    scaled = corr * (8.0 / total)
    empty = jnp.zeros((half, half), jnp.float32)
    upper = jnp.concatenate([empty, scaled], axis=1)
    lower = jnp.concatenate([-scaled.T, empty], axis=1)
    ident = jnp.eye(2 * half, dtype=jnp.float32)
    current = (ident + jnp.concatenate([upper, lower], axis=0)) * (1.5 / math.sqrt(65.0))
    for _ in range(NS_ITERS):
        inner = jnp.dot(current.T, current, precision=lax.Precision.HIGHEST)
        current = 1.5 * current - 0.5 * jnp.dot(current, inner, precision=lax.Precision.HIGHEST)
    return current.astype(jnp.bfloat16)

def reference(latent):
    blocks = latent.reshape(ROWS, NPOS, 2 * BLK).transpose(1, 0, 2)

    def one_position(window):
        gram = jnp.dot(window.T, window, preferred_element_type=jnp.float32)
        rotor = orthogonal(jnp.diagonal(gram), gram[:BLK, BLK:])
        return jnp.dot(window, rotor, preferred_element_type=jnp.float32).astype(jnp.bfloat16)
    for _ in range(ROUNDS):
        rotated = lax.map(one_position, blocks)
        blocks = jnp.concatenate([jnp.roll(rotated[:, :, :BLK], 1, axis=0), jnp.roll(rotated[:, :, BLK:], -1, axis=0)], axis=2)
    return blocks.transpose(1, 0, 2).reshape(ROWS, COLS)
```

```python
import functools
import math

import jax
import jax.numpy as jnp
import numpy as np
from jax import lax
from jax.experimental import pallas as pl
from jax.experimental.pallas import tpu as pltpu
from jax.sharding import PartitionSpec as P


F32, BF16 = jnp.float32, jnp.bfloat16
LANES = 128


def polar_coefficients():
    c = 1.5 / math.sqrt(65.0)
    mul, sub = np.polynomial.polynomial.polymul, np.polynomial.polynomial.polysub
    n = np.array([c * c, c * c])
    u = np.array([1.5 - 0.5 * c * c, -0.5 * c * c])
    return [float(v) for v in c * sub(1.5 * u, 0.5 * mul(n, mul(u, mul(u, u))))]


COEF = polar_coefficients()


def window(half):
    return -(-half // LANES) * LANES


def dot(a, b, contract):
    return lax.dot_general(a, b, ((contract[:1], contract[1:]), ((), ())), preferred_element_type=F32)


def low(a):
    return a.astype(BF16)


def stats_rows(left, right):
    row = lax.broadcasted_iota(jnp.int32, (16, left.shape[1]), 0)
    return jnp.where(row == 0, left, jnp.where(row == 1, right, 0.0))


def gram_kernel(x_ref, g_ref, acc, sq):
    step, last = pl.program_id(0), pl.num_programs(0) - 1
    half = x_ref.shape[1] // 2
    w = acc.shape[1]
    x = x_ref[...]
    part = dot(x[:, :w], x[:, 2 * half - w :], (0, 0))
    xf = x.astype(F32)
    norm = jnp.sum(xf * xf, axis=0, keepdims=True)

    @pl.when(step == 0)
    def _():
        acc[...] = part
        sq[...] = norm

    @pl.when(step > 0)
    def _():
        acc[...] += part
        sq[...] += norm

    @pl.when(step == last)
    def _():
        g_ref[:half] = low(acc[:half])
        s = sq[...]
        g_ref[half:] = low(stats_rows(s[:, :w], s[:, 2 * half - w :]))


def gram(x, tile):
    rows, cols = x.shape
    half = cols // 2
    w = window(half)
    return pl.pallas_call(
        gram_kernel,
        grid=(rows // tile,),
        in_specs=[pl.BlockSpec((tile, cols), lambda i: (i, 0))],
        out_specs=pl.BlockSpec((half + 16, w), lambda i: (0, 0)),
        out_shape=jax.ShapeDtypeStruct((half + 16, w), BF16),
        scratch_shapes=[pltpu.VMEM((w, w), F32), pltpu.VMEM((1, cols), F32)],
        cost_estimate=pl.CostEstimate(flops=2 * rows * w * w, bytes_accessed=2 * rows * cols, transcendentals=0),
        name="gram",
    )(x)


def gram_pair_kernel(half, a_ref, b_ref, g_ref, top, bot, sa, sb):
    step, last = pl.program_id(0), pl.num_programs(0) - 1
    w = top.shape[1]
    pad = w - half
    a, b = a_ref[...], b_ref[...]
    p_top = dot(a[:, :w], b[:, :w], (0, 0))
    p_bot = dot(a[:, 2 * half - w :], b[:, 2 * half - w :], (0, 0))
    af, bf = a.astype(F32), b.astype(F32)
    n_a = jnp.sum(af * af, axis=0, keepdims=True)
    n_b = jnp.sum(bf * bf, axis=0, keepdims=True)

    @pl.when(step == 0)
    def _():
        top[...] = p_top
        bot[...] = p_bot
        sa[...] = n_a
        sb[...] = n_b

    @pl.when(step > 0)
    def _():
        top[...] += p_top
        bot[...] += p_bot
        sa[...] += n_a
        sb[...] += n_b

    @pl.when(step == last)
    def _():
        g_ref[:half] = low(pltpu.roll(top[:half], pad, 1) + bot[pad:])
        s, t = sa[...], sb[...]
        s8, t8 = jnp.broadcast_to(s, (8, 2 * half)), jnp.broadcast_to(t, (8, 2 * half))
        left = s8[:, :w] + pltpu.roll(s8[:, 2 * half - w :], half, 1)
        right = pltpu.roll(t8[:, :w], pad, 1) + t8[:, 2 * half - w :]
        g_ref[half:] = low(stats_rows(left[:1], right[:1]))


def gram_pair(a, b, tile):
    rows, cols = a.shape
    half = cols // 2
    w = window(half)
    return pl.pallas_call(
        functools.partial(gram_pair_kernel, half),
        grid=(rows // tile,),
        in_specs=[pl.BlockSpec((tile, cols), lambda i: (i, 0))] * 2,
        out_specs=pl.BlockSpec((half + 16, w), lambda i: (0, 0)),
        out_shape=jax.ShapeDtypeStruct((half + 16, w), BF16),
        scratch_shapes=[pltpu.VMEM((w, w), F32)] * 2 + [pltpu.VMEM((1, cols), F32)] * 2,
        cost_estimate=pl.CostEstimate(flops=4 * rows * w * w, bytes_accessed=4 * rows * cols, transcendentals=0),
        name="gram_pair",
    )(a, b)


def cross_of(parts):
    total = sum((p[...].astype(F32) for p in parts[1:]), parts[0][...].astype(F32))
    w = total.shape[1]
    half = total.shape[0] - 16
    pad = w - half
    norms = total[half : half + 8]
    left = jnp.transpose(norms)[:half, :1]
    corr = total[:half] * (lax.rsqrt(left) * lax.rsqrt(norms[1:2]))
    lane = lax.broadcasted_iota(jnp.int32, corr.shape, 1)
    corr = jnp.where(lane >= pad, corr, 0.0)
    size = jnp.sqrt(2.0 * jnp.sum(corr * corr) + 1e-12)
    scaled = corr * (8.0 / size)
    return jnp.concatenate([scaled, jnp.zeros((pad, w), F32)], axis=0)


def minus_constant(k, k2):
    return COEF[1] * k + COEF[2] * k2 + dot(low(k2), low(COEF[3] * k + COEF[4] * k2), (1, 0))


def eye_at(w, first, stop):
    r = lax.broadcasted_iota(jnp.int32, (w, w), 0)
    c = lax.broadcasted_iota(jnp.int32, (w, w), 1)
    return (r == c) & (r >= first) & (r < stop)


def left_columns(x, half):
    w = x.shape[1]
    xb = low(x)
    k = dot(xb, xb, (1, 1))
    delta = minus_constant(k, dot(low(k), low(k), (1, 0)))
    upper = delta + jnp.where(eye_at(w, 0, half), COEF[0], 0.0)
    lower = -(COEF[0] * jnp.transpose(x) + dot(xb, low(delta), (0, 0)))
    return low(jnp.concatenate([upper[:half], lower[w - half :]], axis=0))


def right_columns(x, half):
    w = x.shape[1]
    xb = low(x)
    k = dot(xb, xb, (0, 0))
    delta = minus_constant(k, dot(low(k), low(k), (1, 0)))
    upper = COEF[0] * x + dot(xb, low(delta), (1, 0))
    lower = delta + jnp.where(eye_at(w, w - half, w), COEF[0], 0.0)
    return low(jnp.concatenate([upper[:half], lower[w - half :]], axis=0))


def moved(q, by):
    return low(pltpu.roll(q.astype(F32), by, 1)) if by else q


def packed_store(ref, rows, top, bot, half):
    w = top.shape[1]
    o = 2 * half - w
    ref[rows, :o] = low(top[:, :o])
    if w > o:
        ref[rows, o:w] = low(top[:, o:] + bot[:, : w - o])
    ref[rows, w:] = low(bot[:, w - o :])


def rotor_kernel(n_parts, tile, *refs):
    parts = refs[:n_parts]
    x_hbm, a_ref, r0_ref, r1_ref, x_ref, sem = refs[n_parts:]
    half = x_ref.shape[1] // 2
    w = parts[0].shape[1]
    copy = pltpu.make_async_copy(x_hbm, x_ref, sem)
    copy.start()
    x = cross_of(parts)
    left = left_columns(x, half)
    left_end = moved(left, w - half)
    copy.wait()
    rows = a_ref.shape[0]

    @pl.loop(0, rows // tile)
    def _(i):
        here = pl.ds(pl.multiple_of(i * tile, tile), tile)
        there = pl.ds(pl.multiple_of(rows + i * tile, tile), tile)
        top = dot(x_ref[here, :], left, (1, 0))
        bot = dot(x_ref[there, :], left_end, (1, 0))
        packed_store(a_ref, here, top, bot, half)

    right = right_columns(x, half)
    r0_ref[...] = moved(right, half)
    r1_ref[...] = right


def rotor(parts, x, tile):
    rows, cols = x.shape
    half = cols // 2
    w = parts[0].shape[1]
    return pl.pallas_call(
        functools.partial(rotor_kernel, len(parts), tile),
        in_specs=[pl.BlockSpec(memory_space=pltpu.VMEM)] * len(parts) + [pl.BlockSpec(memory_space=pl.ANY)],
        out_specs=[pl.BlockSpec(memory_space=pltpu.VMEM)] * 3,
        out_shape=[
            jax.ShapeDtypeStruct((rows // 2, cols), BF16),
            jax.ShapeDtypeStruct((cols, w), BF16),
            jax.ShapeDtypeStruct((cols, w), BF16),
        ],
        scratch_shapes=[pltpu.VMEM((rows, cols), BF16), pltpu.SemaphoreType.DMA],
        cost_estimate=pl.CostEstimate(flops=2 * rows * cols * w, bytes_accessed=3 * rows * cols, transcendentals=0),
        name="rotor",
    )(*parts, x)


def rotate_kernel(half, t_ref, b_ref, q0_ref, q1_ref, o_ref):
    top = dot(t_ref[...], q0_ref[...], (1, 0))
    bot = dot(b_ref[...], q1_ref[...], (1, 0))
    packed_store(o_ref, slice(None), top, bot, half)


def rotate(x, q0, q1, tile):
    rows, cols = x.shape
    w = q0.shape[1]
    steps = rows // 2 // tile
    return pl.pallas_call(
        functools.partial(rotate_kernel, cols // 2),
        grid=(steps,),
        in_specs=[
            pl.BlockSpec((tile, cols), lambda i: (i, 0)),
            pl.BlockSpec((tile, cols), lambda i: (i + steps, 0)),
            pl.BlockSpec((cols, w), lambda i: (0, 0)),
            pl.BlockSpec((cols, w), lambda i: (0, 0)),
        ],
        out_specs=pl.BlockSpec((tile, cols), lambda i: (i, 0)),
        out_shape=jax.ShapeDtypeStruct((rows // 2, cols), BF16),
        cost_estimate=pl.CostEstimate(flops=2 * rows * cols * w, bytes_accessed=3 * rows * cols, transcendentals=0),
        name="rotate",
    )(x, x, q0, q1)


def second_kernel(n_parts, *refs):
    parts = refs[:n_parts]
    x_ref, left_ref = refs[n_parts:]
    half = parts[0].shape[0] - 16
    x = cross_of(parts)
    x_ref[...] = low(x[:half])
    left_ref[...] = left_columns(x, half)


def second(parts):
    half = parts[0].shape[0] - 16
    w = parts[0].shape[1]
    return pl.pallas_call(
        functools.partial(second_kernel, len(parts)),
        in_specs=[pl.BlockSpec(memory_space=pltpu.VMEM)] * len(parts),
        out_specs=[pl.BlockSpec(memory_space=pltpu.VMEM)] * 2,
        out_shape=[jax.ShapeDtypeStruct((half, w), BF16), jax.ShapeDtypeStruct((2 * half, w), BF16)],
        cost_estimate=pl.CostEstimate(flops=8 * w**3, bytes_accessed=4 * w * w, transcendentals=0),
        name="second",
    )(*parts)


def right_kernel(x_ref, right_ref):
    half, w = x_ref.shape
    x = jnp.concatenate([x_ref[...].astype(F32), jnp.zeros((w - half, w), F32)], axis=0)
    right_ref[...] = right_columns(x, half)


def right_of(x):
    half, w = x.shape
    return pl.pallas_call(
        right_kernel,
        in_specs=[pl.BlockSpec(memory_space=pltpu.VMEM)],
        out_specs=pl.BlockSpec(memory_space=pltpu.VMEM),
        out_shape=jax.ShapeDtypeStruct((2 * half, w), BF16),
        cost_estimate=pl.CostEstimate(flops=8 * w**3, bytes_accessed=4 * w * w, transcendentals=0),
        name="right",
    )(x)


def final_kernel(half, ain_ref, b_ref, a_ref, bin_ref, left_ref, right_ref, o_ref):
    w = left_ref.shape[1]
    o = 2 * half - w
    low_half = pl.program_id(0) == 0
    rest = jnp.zeros((w - half, w), BF16)

    def emit(first):
        cols = slice(0, w) if first else slice(o, 2 * half)

        def weight(q_ref, lower):
            q = q_ref[half:] if lower else q_ref[:half]
            return jnp.concatenate([q, rest] if first else [rest, q], axis=0)

        l = dot(ain_ref[:, cols], weight(left_ref, False), (1, 0)) + dot(b_ref[:, cols], weight(left_ref, True), (1, 0))
        r = dot(a_ref[:, cols], weight(right_ref, False), (1, 0)) + dot(bin_ref[:, cols], weight(right_ref, True), (1, 0))
        packed_store(o_ref, slice(None), l, r, half)

    pl.when(low_half)(lambda: emit(True))
    pl.when(jnp.logical_not(low_half))(lambda: emit(False))


def final(ain, b, a, bin_, left, right, tile):
    rows, cols = a.shape
    w = left.shape[1]
    steps = rows // tile
    block = pl.BlockSpec((tile, cols), lambda h, i: (i, 0))
    return pl.pallas_call(
        functools.partial(final_kernel, cols // 2),
        grid=(2, steps),
        in_specs=[block] * 4 + [pl.BlockSpec((cols, w), lambda h, i: (0, 0))] * 2,
        out_specs=pl.BlockSpec((tile, cols), lambda h, i: (h * steps + i, 0)),
        out_shape=jax.ShapeDtypeStruct((2 * rows, cols), BF16),
        cost_estimate=pl.CostEstimate(flops=16 * rows * w * w, bytes_accessed=12 * rows * cols, transcendentals=0),
        name="final",
    )(ain, b, a, bin_, left, right)


def shifted(x, axis, by):
    n = lax.axis_size(axis)
    return lax.ppermute(x, axis, [(i, (i + by) % n) for i in range(n)])


def row_parts(g):
    n = lax.axis_size("rows")
    if n & (n - 1) or n > 4:
        return [lax.psum(g.astype(F32), "rows")]
    return [g] + [lax.ppermute(g, "rows", [(i, i ^ k) for i in range(n)]) for k in range(1, n)]


def local(latent):
    tile = 256
    parts = row_parts(gram(latent, 2 * tile))
    a, r0, r1 = rotor(parts, latent, tile)
    a_in = shifted(a, "pairs", 2)
    b = rotate(latent, r0, r1, tile)
    a_in, b_out = lax.optimization_barrier((a_in, b))
    b_in = shifted(b_out, "pairs", -2)
    parts = row_parts(gram_pair(a_in, b, tile))
    x, left = second(parts)
    right = right_of(shifted(x, "pairs", -2))
    return final(a_in, b, a, b_in, left, right, tile)


def solution(mesh):
    return jax.shard_map(
        local,
        mesh=mesh,
        in_specs=(P("rows", "pairs"),),
        out_specs=P("rows", "pairs"),
        check_vma=False,
    )
```

```python
import functools
import math

import jax
import jax.numpy as jnp
import numpy as np
from jax import lax
from jax.experimental import pallas as pl
from jax.experimental.pallas import tpu as pltpu
from jax.sharding import PartitionSpec as P


F32, BF16 = jnp.float32, jnp.bfloat16
LANES = 128


def polar_coefficients():
    c = 1.5 / math.sqrt(65.0)
    mul, sub = np.polynomial.polynomial.polymul, np.polynomial.polynomial.polysub
    n = np.array([c * c, c * c])
    u = np.array([1.5 - 0.5 * c * c, -0.5 * c * c])
    return [float(v) for v in c * sub(1.5 * u, 0.5 * mul(n, mul(u, mul(u, u))))]


COEF = polar_coefficients()


def window(half):
    return -(-half // LANES) * LANES


def dot(a, b, contract):
    return lax.dot_general(a, b, ((contract[:1], contract[1:]), ((), ())), preferred_element_type=F32)


def low(a):
    return a.astype(BF16)


def params():
    return pltpu.CompilerParams(vmem_limit_bytes=16 << 20)


def whole(n):
    return [pl.BlockSpec(memory_space=pltpu.VMEM)] * n


def pieces(rows, n):
    return [slice(i * (rows // n), (i + 1) * (rows // n)) for i in range(n)]


def spans(*lists):
    cuts = {0}
    for blocks in lists:
        stop = 0
        for block in blocks:
            stop += block.shape[0]
            cuts.add(stop)
    cuts = sorted(cuts)
    return list(zip(cuts[:-1], cuts[1:]))


def span(blocks, start, stop):
    for block in blocks:
        if start < block.shape[0]:
            return block.at[start:stop]
        start, stop = start - block.shape[0], stop - block.shape[0]


def blocks_of(cols, sizes):
    return [jax.ShapeDtypeStruct((n, cols), BF16) for n in sizes]


def pack_window(top, bot, half):
    w = top.shape[1]
    lane = lax.broadcasted_iota(jnp.int32, top.shape, 1)
    return jnp.where(lane < half, pltpu.roll(top, half, 1), 0.0), jnp.where(lane >= w - half, bot, 0.0)


def unpack_window(packed):
    cols = packed.shape[1]
    half = cols // 2
    w = window(half)
    return jnp.concatenate([pltpu.roll(packed[:, :w], w - half, 1), packed[:, cols - w :]], axis=0)


def pack_stats(g_ref, cross, norms):
    half, _ = cross.shape
    h = half // 2
    packed_store(g_ref, slice(0, h), *pack_window(cross[:h], cross[h:], half), half)
    row = lax.broadcasted_iota(jnp.int32, (8, g_ref.shape[1]), 0)
    g_ref[h:] = low(jnp.where(row == 0, norms, 0.0))


def stats_shape(cols):
    return jax.ShapeDtypeStruct((cols // 4 + 8, cols), BF16)


def gram_kernel(n, x_hbm, g_ref, x_ref, sem):
    rows, cols = x_ref.shape
    half = cols // 2
    w = window(half)
    copies = [
        pltpu.make_async_copy(x_hbm.at[r, :], x_ref.at[r, :], sem.at[i]) for i, r in enumerate(pieces(rows, n))
    ]
    for copy in copies:
        copy.start()
    cross, norms = jnp.zeros((w, w), F32), jnp.zeros((1, cols), F32)
    for copy, r in zip(copies, pieces(rows, n)):
        copy.wait()
        x = x_ref[r, :]
        cross += dot(x[:, :w], x[:, cols - w :], (0, 0))
        xf = x.astype(F32)
        norms += jnp.sum(xf * xf, axis=0, keepdims=True)
    pack_stats(g_ref, cross[:half], norms)


def gram(x, n):
    rows, cols = x.shape
    w = window(cols // 2)
    x = pltpu.with_memory_space_constraint(x, pltpu.HBM)
    return pl.pallas_call(
        functools.partial(gram_kernel, n),
        in_specs=[pl.BlockSpec(memory_space=pltpu.HBM)],
        out_specs=whole(2),
        out_shape=[stats_shape(cols), jax.ShapeDtypeStruct((rows, cols), BF16)],
        scratch_shapes=[pltpu.SemaphoreType.DMA((n,))],
        cost_estimate=pl.CostEstimate(flops=2 * rows * w * w, bytes_accessed=2 * rows * cols, transcendentals=0),
        compiler_params=params(),
        name="gram",
    )(x)


def gram_pair_kernel(n_a, *refs):
    a_refs, b_refs, g_ref = refs[:n_a], refs[n_a:-1], refs[-1]
    cols = g_ref.shape[1]
    half = cols // 2
    w = window(half)
    pad, o = w - half, cols - w
    top, bot = jnp.zeros((w, w), F32), jnp.zeros((w, w), F32)
    norm_a, norm_b = jnp.zeros((1, cols), F32), jnp.zeros((1, cols), F32)
    for start, stop in spans(a_refs, b_refs):
        a, b = span(a_refs, start, stop)[...], span(b_refs, start, stop)[...]
        top += dot(a[:, :w], b[:, :w], (0, 0))
        bot += dot(a[:, o:], b[:, o:], (0, 0))
        af, bf = a.astype(F32), b.astype(F32)
        norm_a += jnp.sum(af * af, axis=0, keepdims=True)
        norm_b += jnp.sum(bf * bf, axis=0, keepdims=True)
    cross = pltpu.roll(top[:half], pad, 1) + bot[pad:]
    s, t = jnp.broadcast_to(norm_a, (8, cols)), jnp.broadcast_to(norm_b, (8, cols))
    left = s + jnp.concatenate([pltpu.roll(s[:, o:], half, 1), jnp.zeros((8, o), F32)], axis=1)
    right = t + jnp.concatenate([jnp.zeros((8, o), F32), pltpu.roll(t[:, :w], pad, 1)], axis=1)
    lane = lax.broadcasted_iota(jnp.int32, (8, cols), 1)
    pack_stats(g_ref, cross, jnp.where(lane < half, left, right)[:1])


def gram_pair(a, b):
    cols = a[0].shape[1]
    rows = sum(v.shape[0] for v in a)
    w = window(cols // 2)
    return pl.pallas_call(
        functools.partial(gram_pair_kernel, len(a)),
        in_specs=whole(len(a) + len(b)),
        out_specs=whole(1)[0],
        out_shape=stats_shape(cols),
        cost_estimate=pl.CostEstimate(flops=4 * rows * w * w, bytes_accessed=4 * rows * cols, transcendentals=0),
        compiler_params=params(),
        name="gram_pair",
    )(*a, *b)


def cross_of(parts):
    total = sum((p[...].astype(F32) for p in parts[1:]), parts[0][...].astype(F32))
    cols = total.shape[1]
    half = cols // 2
    w = window(half)
    pad, h = w - half, half // 2
    cross = unpack_window(total[:h])
    norms = total[h:]
    left = jnp.transpose(norms[:, :w])[:half, :1]
    corr = cross * (lax.rsqrt(left) * lax.rsqrt(norms[:1, cols - w :]))
    lane = lax.broadcasted_iota(jnp.int32, corr.shape, 1)
    corr = jnp.where(lane >= pad, corr, 0.0)
    size = jnp.sqrt(2.0 * jnp.sum(corr * corr) + 1e-12)
    return filled(corr * (8.0 / size))


def filled(x):
    half, w = x.shape
    return jnp.concatenate([x, jnp.zeros((w - half, w), F32)], axis=0) if w > half else x


def minus_constant(k, k2):
    return COEF[1] * k + COEF[2] * k2 + dot(low(k2), low(COEF[3] * k + COEF[4] * k2), (1, 0))


def eye_at(w, first, stop):
    r = lax.broadcasted_iota(jnp.int32, (w, w), 0)
    c = lax.broadcasted_iota(jnp.int32, (w, w), 1)
    return (r == c) & (r >= first) & (r < stop)


def left_columns(x, half):
    w = x.shape[1]
    xb = low(x)
    k = dot(xb, xb, (1, 1))
    delta = minus_constant(k, dot(low(k), low(k), (1, 0)))
    upper = delta + jnp.where(eye_at(w, 0, half), COEF[0], 0.0)
    lower = -(COEF[0] * jnp.transpose(x) + dot(xb, low(delta), (0, 0)))
    return low(jnp.concatenate([upper[:half], lower[w - half :]], axis=0))


def right_columns(x, half):
    w = x.shape[1]
    xb = low(x)
    k = dot(xb, xb, (0, 0))
    delta = minus_constant(k, dot(low(k), low(k), (1, 0)))
    upper = COEF[0] * x + dot(xb, low(delta), (1, 0))
    lower = delta + jnp.where(eye_at(w, w - half, w), COEF[0], 0.0)
    return low(jnp.concatenate([upper[:half], lower[w - half :]], axis=0))


def moved(q, by):
    return low(pltpu.roll(q.astype(F32), by, 1)) if by else q


def packed_store(ref, rows, top, bot, half):
    w = top.shape[1]
    o = 2 * half - w
    ref[rows, :o] = low(top[:, :o])
    if w > o:
        ref[rows, o:w] = low(top[:, o:] + bot[:, : w - o])
    ref[rows, w:] = low(bot[:, w - o :])


def rotate_into(refs, x_ref, q_top, q_bot):
    rows = sum(ref.shape[0] for ref in refs)
    half = x_ref.shape[1] // 2
    for start, stop in spans(refs):
        top = dot(x_ref[start:stop, :], q_top, (1, 0))
        bot = dot(x_ref[rows + start : rows + stop, :], q_bot, (1, 0))
        packed_store(span(refs, start, stop), slice(None), top, bot, half)


def rotor_kernel(n_parts, *refs):
    parts = refs[:n_parts]
    x_ref, s_ref, *a_refs = refs[n_parts:]
    half = s_ref.shape[0]
    s = cross_of(parts)
    left = left_columns(s, half)
    rotate_into(a_refs, x_ref, left, moved(left, s.shape[1] - half))
    s_ref[...] = s[:half]


def rotor(parts, x, sizes):
    rows, cols = x.shape
    w = window(cols // 2)
    s, *a = pl.pallas_call(
        functools.partial(rotor_kernel, len(parts)),
        in_specs=whole(len(parts) + 1),
        out_specs=whole(1 + len(sizes)),
        out_shape=[jax.ShapeDtypeStruct((cols // 2, w), F32)] + blocks_of(cols, sizes),
        cost_estimate=pl.CostEstimate(flops=2 * rows * cols * w, bytes_accessed=3 * rows * cols, transcendentals=0),
        compiler_params=params(),
        name="rotor",
    )(*parts, x)
    return s, a


def rotate_kernel(s_ref, x_ref, *b_refs):
    half = s_ref.shape[0]
    right = right_columns(filled(s_ref[...]), half)
    rotate_into(b_refs, x_ref, moved(right, half), right)


def rotate(s, x, sizes):
    rows, cols = x.shape
    w = s.shape[1]
    return pl.pallas_call(
        rotate_kernel,
        in_specs=whole(2),
        out_specs=whole(len(sizes)),
        out_shape=blocks_of(cols, sizes),
        cost_estimate=pl.CostEstimate(flops=2 * rows * cols * w, bytes_accessed=3 * rows * cols, transcendentals=0),
        compiler_params=params(),
        name="rotate",
    )(s, x)


def second_kernel(n_parts, *refs):
    parts = refs[:n_parts]
    s_ref, left_ref = refs[n_parts:]
    h, cols = s_ref.shape
    s = cross_of(parts)
    packed_store(s_ref, slice(None), *pack_window(s[:h], s[h : 2 * h], cols // 2), cols // 2)
    left_ref[...] = left_columns(s, cols // 2)


def second(parts):
    cols = parts[0].shape[1]
    w = window(cols // 2)
    return pl.pallas_call(
        functools.partial(second_kernel, len(parts)),
        in_specs=whole(len(parts)),
        out_specs=whole(2),
        out_shape=[jax.ShapeDtypeStruct((cols // 4, cols), BF16), jax.ShapeDtypeStruct((cols, w), BF16)],
        cost_estimate=pl.CostEstimate(flops=8 * w**3, bytes_accessed=4 * w * w, transcendentals=0),
        compiler_params=params(),
        name="second",
    )(*parts)


def right_kernel(s_ref, right_ref):
    s = unpack_window(s_ref[...].astype(F32))
    half, w = s.shape
    lane = lax.broadcasted_iota(jnp.int32, s.shape, 1)
    right_ref[...] = right_columns(filled(jnp.where(lane >= w - half, s, 0.0)), half)


def right_of(s):
    cols = s.shape[1]
    w = window(cols // 2)
    return pl.pallas_call(
        right_kernel,
        in_specs=whole(1),
        out_specs=whole(1)[0],
        out_shape=jax.ShapeDtypeStruct((cols, w), BF16),
        cost_estimate=pl.CostEstimate(flops=8 * w**3, bytes_accessed=4 * w * w, transcendentals=0),
        compiler_params=params(),
        name="right",
    )(s)


def pair_weight(q_ref, first):
    cols, w = q_ref.shape
    half = cols // 2
    rest = jnp.zeros((w - half, w), BF16)
    upper, lower = q_ref[:half], q_ref[half:]
    return jnp.concatenate([upper, rest, lower, rest] if first else [rest, upper, rest, lower], axis=0)


def pair_dot(a_refs, b_refs, start, stop, weight, first):
    w = weight.shape[1]
    cols = a_refs[0].shape[1]
    at = slice(0, w) if first else slice(cols - w, cols)
    a, b = span(a_refs, start, stop)[:, at], span(b_refs, start, stop)[:, at]
    return dot(jnp.concatenate([a, b], axis=1), weight, (1, 0))


def left_kernel(n_a, *refs):
    a_refs, (*b_refs, q_ref, o_ref) = refs[:n_a], refs[n_a:]
    rows = o_ref.shape[0] // 2
    for first in (True, False):
        weight = pair_weight(q_ref, first)
        for start, stop in spans(a_refs, b_refs):
            to = 0 if first else rows
            o_ref[to + start : to + stop, :] = low(pair_dot(a_refs, b_refs, start, stop, weight, first))


def left_half(a, b, q):
    rows, cols = sum(v.shape[0] for v in a), a[0].shape[1]
    w = q.shape[1]
    return pl.pallas_call(
        functools.partial(left_kernel, len(a)),
        in_specs=whole(len(a) + len(b) + 1),
        out_specs=whole(1)[0],
        out_shape=jax.ShapeDtypeStruct((2 * rows, w), BF16),
        cost_estimate=pl.CostEstimate(flops=8 * rows * w * w, bytes_accessed=6 * rows * cols, transcendentals=0),
        compiler_params=params(),
        name="left_half",
    )(*a, *b, q)


def final_kernel(n_a, n_b, *refs):
    a_refs, b_refs, (l_ref, q_ref, o_hbm, o_ref, sem) = refs[:n_a], refs[n_a : n_a + n_b], refs[n_a + n_b :]
    rows, cols = o_ref.shape[0] // 2, o_ref.shape[1]
    copies = []
    for first in (True, False):
        weight = pair_weight(q_ref, first)
        for start, stop in spans(a_refs, b_refs):
            to = slice(start, stop) if first else slice(rows + start, rows + stop)
            right = pair_dot(a_refs, b_refs, start, stop, weight, first)
            packed_store(o_ref, to, l_ref[to, :].astype(F32), right, cols // 2)
            copy = pltpu.make_async_copy(o_ref.at[to, :], o_hbm.at[to, :], sem.at[len(copies)])
            copy.start()
            copies.append(copy)
    for copy in copies:
        copy.wait()


def final(l, a, b, q):
    rows, cols = l.shape[0], a[0].shape[1]
    w = q.shape[1]
    return pl.pallas_call(
        functools.partial(final_kernel, len(a), len(b)),
        in_specs=whole(len(a) + len(b) + 2),
        out_specs=pl.BlockSpec(memory_space=pl.ANY),
        out_shape=jax.ShapeDtypeStruct((rows, cols), BF16),
        scratch_shapes=[pltpu.VMEM((rows, cols), BF16), pltpu.SemaphoreType.DMA((2 * len(spans(a, b)),))],
        cost_estimate=pl.CostEstimate(flops=4 * rows * w * w, bytes_accessed=4 * rows * cols, transcendentals=0),
        compiler_params=params(),
        name="final",
    )(*a, *b, l, q)


def shifted(x, axis, by):
    n = lax.axis_size(axis)
    return lax.ppermute(x, axis, [(i, (i + by) % n) for i in range(n)])


def row_parts(g):
    n = lax.axis_size("rows")
    if n & (n - 1) or n > 4:
        return [lax.psum(g.astype(F32), "rows")]
    return [g] + [lax.ppermute(g, "rows", [(i, i ^ k) for i in range(n)]) for k in range(1, n)]


def shares(rows, *eighths):
    return [rows * e // 8 for e in eighths]


def local(latent):
    rows = latent.shape[0] // 2
    stats, latent = gram(latent, 4)
    s, a = rotor(row_parts(stats), latent, shares(rows, 7, 1))
    a_in = [shifted(v, "pairs", 2) for v in a]
    b = rotate(s, latent, shares(rows, 5, 3))
    a_in[0], b_out = lax.optimization_barrier((a_in[0], b[0]))
    b_in = [shifted(b_out, "pairs", -2)]
    s, left = second(row_parts(gram_pair(a_in, b)))
    s_in = shifted(s, "pairs", -2)
    left, b_out = lax.optimization_barrier((left, b[1]))
    b_in.append(shifted(b_out, "pairs", -2))
    return final(left_half(a_in, b, left), a, b_in, right_of(s_in))


def solution(mesh):
    return jax.shard_map(
        local,
        mesh=mesh,
        in_specs=(P("rows", "pairs"),),
        out_specs=P("rows", "pairs"),
        check_vma=False,
    )
```

```python
import functools
import math

import jax
import jax.numpy as jnp
import numpy as np
from jax import lax
from jax.experimental import pallas as pl
from jax.experimental.pallas import tpu as pltpu
from jax.sharding import PartitionSpec as P


F32, BF16 = jnp.float32, jnp.bfloat16
LANES = 128


def polar_coefficients():
    c = 1.5 / math.sqrt(65.0)
    mul, sub = np.polynomial.polynomial.polymul, np.polynomial.polynomial.polysub
    n = np.array([c * c, c * c])
    u = np.array([1.5 - 0.5 * c * c, -0.5 * c * c])
    return [float(v) for v in c * sub(1.5 * u, 0.5 * mul(n, mul(u, mul(u, u))))]


COEF = polar_coefficients()


def window(half):
    return -(-half // LANES) * LANES


def dot(a, b, contract):
    return lax.dot_general(a, b, ((contract[:1], contract[1:]), ((), ())), preferred_element_type=F32)


def low(a):
    return a.astype(BF16)


def params():
    return pltpu.CompilerParams(vmem_limit_bytes=16 << 20)


def whole(n):
    return [pl.BlockSpec(memory_space=pltpu.VMEM)] * n


def pieces(rows, n):
    return [slice(i * (rows // n), (i + 1) * (rows // n)) for i in range(n)]


def spans(*lists):
    cuts = {0}
    for blocks in lists:
        stop = 0
        for block in blocks:
            stop += block.shape[0]
            cuts.add(stop)
    cuts = sorted(cuts)
    return list(zip(cuts[:-1], cuts[1:]))


def span(blocks, start, stop):
    for block in blocks:
        if start < block.shape[0]:
            return block.at[start:stop]
        start, stop = start - block.shape[0], stop - block.shape[0]


def blocks_of(cols, sizes):
    return [jax.ShapeDtypeStruct((n, cols), BF16) for n in sizes]


def pack_window(top, bot, half):
    w = top.shape[1]
    lane = lax.broadcasted_iota(jnp.int32, top.shape, 1)
    return jnp.where(lane < half, pltpu.roll(top, half, 1), 0.0), jnp.where(lane >= w - half, bot, 0.0)


def unpack_window(packed):
    cols = packed.shape[1]
    half = cols // 2
    w = window(half)
    return jnp.concatenate([pltpu.roll(packed[:, :w], w - half, 1), packed[:, cols - w :]], axis=0)


def pack_stats(g_ref, cross, norms):
    half, _ = cross.shape
    h = half // 2
    packed_store(g_ref, slice(0, h), *pack_window(cross[:h], cross[h:], half), half)
    row = lax.broadcasted_iota(jnp.int32, (8, g_ref.shape[1]), 0)
    g_ref[h:] = low(jnp.where(row == 0, norms, 0.0))


def stats_shape(cols):
    return jax.ShapeDtypeStruct((cols // 4 + 8, cols), BF16)


def taken_kernel(x_hbm, raw_ref, sem):
    rows, k = x_hbm.shape[0], raw_ref.shape[0] // 2
    copies = [
        pltpu.make_async_copy(x_hbm.at[stop - k : stop, :], raw_ref.at[i * k : (i + 1) * k, :], sem.at[i])
        for i, stop in enumerate((rows // 2, rows))
    ]
    for copy in copies:
        copy.start()
    for copy in copies:
        copy.wait()


def taken(x, k):
    cols = x.shape[1]
    return pl.pallas_call(
        taken_kernel,
        in_specs=[pl.BlockSpec(memory_space=pltpu.HBM)],
        out_specs=whole(1)[0],
        out_shape=jax.ShapeDtypeStruct((2 * k, cols), BF16),
        scratch_shapes=[pltpu.SemaphoreType.DMA((2,))],
        cost_estimate=pl.CostEstimate(flops=0, bytes_accessed=8 * k * cols, transcendentals=0),
        compiler_params=params(),
        name="taken",
    )(pltpu.with_memory_space_constraint(x, pltpu.HBM))


def gram_kernel(n, x_ref, g_ref):
    rows, cols = x_ref.shape
    half = cols // 2
    w = window(half)
    cross, norms = jnp.zeros((w, w), F32), jnp.zeros((1, cols), F32)
    for r in pieces(rows, n):
        x = x_ref[r, :]
        cross += dot(x[:, :w], x[:, cols - w :], (0, 0))
        xf = x.astype(F32)
        norms += jnp.sum(xf * xf, axis=0, keepdims=True)
    pack_stats(g_ref, cross[:half], norms)


def gram(x, n):
    rows, cols = x.shape
    w = window(cols // 2)
    return pl.pallas_call(
        functools.partial(gram_kernel, n),
        in_specs=whole(1),
        out_specs=whole(1)[0],
        out_shape=stats_shape(cols),
        cost_estimate=pl.CostEstimate(flops=2 * rows * w * w, bytes_accessed=2 * rows * cols, transcendentals=0),
        compiler_params=params(),
        name="gram",
    )(x)


def gram_pair_kernel(n_a, *refs):
    a_refs, b_refs, g_ref = refs[:n_a], refs[n_a:-1], refs[-1]
    cols = g_ref.shape[1]
    half = cols // 2
    w = window(half)
    pad, o = w - half, cols - w
    top, bot = jnp.zeros((w, w), F32), jnp.zeros((w, w), F32)
    norm_a, norm_b = jnp.zeros((1, cols), F32), jnp.zeros((1, cols), F32)
    for start, stop in spans(a_refs, b_refs):
        a, b = span(a_refs, start, stop)[...], span(b_refs, start, stop)[...]
        top += dot(a[:, :w], b[:, :w], (0, 0))
        bot += dot(a[:, o:], b[:, o:], (0, 0))
        af, bf = a.astype(F32), b.astype(F32)
        norm_a += jnp.sum(af * af, axis=0, keepdims=True)
        norm_b += jnp.sum(bf * bf, axis=0, keepdims=True)
    cross = pltpu.roll(top[:half], pad, 1) + bot[pad:]
    s, t = jnp.broadcast_to(norm_a, (8, cols)), jnp.broadcast_to(norm_b, (8, cols))
    left = s + jnp.concatenate([pltpu.roll(s[:, o:], half, 1), jnp.zeros((8, o), F32)], axis=1)
    right = t + jnp.concatenate([jnp.zeros((8, o), F32), pltpu.roll(t[:, :w], pad, 1)], axis=1)
    lane = lax.broadcasted_iota(jnp.int32, (8, cols), 1)
    pack_stats(g_ref, cross, jnp.where(lane < half, left, right)[:1])


def gram_pair(a, b):
    cols = a[0].shape[1]
    rows = sum(v.shape[0] for v in a)
    w = window(cols // 2)
    return pl.pallas_call(
        functools.partial(gram_pair_kernel, len(a)),
        in_specs=whole(len(a) + len(b)),
        out_specs=whole(1)[0],
        out_shape=stats_shape(cols),
        cost_estimate=pl.CostEstimate(flops=4 * rows * w * w, bytes_accessed=4 * rows * cols, transcendentals=0),
        compiler_params=params(),
        name="gram_pair",
    )(*a, *b)


def cross_of(parts):
    total = sum((p[...].astype(F32) for p in parts[1:]), parts[0][...].astype(F32))
    cols = total.shape[1]
    half = cols // 2
    w = window(half)
    pad, h = w - half, half // 2
    cross = unpack_window(total[:h])
    norms = total[h:]
    left = jnp.transpose(norms[:, :w])[:half, :1]
    corr = cross * (lax.rsqrt(left) * lax.rsqrt(norms[:1, cols - w :]))
    lane = lax.broadcasted_iota(jnp.int32, corr.shape, 1)
    corr = jnp.where(lane >= pad, corr, 0.0)
    size = jnp.sqrt(2.0 * jnp.sum(corr * corr) + 1e-12)
    return filled(corr * (8.0 / size))


def filled(x):
    half, w = x.shape
    return jnp.concatenate([x, jnp.zeros((w - half, w), F32)], axis=0) if w > half else x


def minus_constant(k, k2):
    return COEF[1] * k + COEF[2] * k2 + dot(low(k2), low(COEF[3] * k + COEF[4] * k2), (1, 0))


def eye_at(w, first, stop):
    r = lax.broadcasted_iota(jnp.int32, (w, w), 0)
    c = lax.broadcasted_iota(jnp.int32, (w, w), 1)
    return (r == c) & (r >= first) & (r < stop)


def left_columns(x, half):
    w = x.shape[1]
    xb = low(x)
    k = dot(xb, xb, (1, 1))
    delta = minus_constant(k, dot(low(k), low(k), (1, 0)))
    upper = delta + jnp.where(eye_at(w, 0, half), COEF[0], 0.0)
    lower = -(COEF[0] * jnp.transpose(x) + dot(xb, low(delta), (0, 0)))
    return low(jnp.concatenate([upper[:half], lower[w - half :]], axis=0))


def right_columns(x, half):
    w = x.shape[1]
    xb = low(x)
    k = dot(xb, xb, (0, 0))
    delta = minus_constant(k, dot(low(k), low(k), (1, 0)))
    upper = COEF[0] * x + dot(xb, low(delta), (1, 0))
    lower = delta + jnp.where(eye_at(w, w - half, w), COEF[0], 0.0)
    return low(jnp.concatenate([upper[:half], lower[w - half :]], axis=0))


def moved(q, by):
    return low(pltpu.roll(q.astype(F32), by, 1)) if by else q


def packed_store(ref, rows, top, bot, half):
    w = top.shape[1]
    o = 2 * half - w
    ref[rows, :o] = low(top[:, :o])
    if w > o:
        ref[rows, o:w] = low(top[:, o:] + bot[:, : w - o])
    ref[rows, w:] = low(bot[:, w - o :])


def rotate_into(refs, x_ref, q_top, q_bot, base=0):
    rows, half = x_ref.shape[0] // 2, x_ref.shape[1] // 2
    for start, stop in spans(refs):
        top = dot(x_ref[base + start : base + stop, :], q_top, (1, 0))
        bot = dot(x_ref[rows + base + start : rows + base + stop, :], q_bot, (1, 0))
        packed_store(span(refs, start, stop), slice(None), top, bot, half)


def rounded_factor(s_ref, s):
    h, cols = s_ref.shape
    packed_store(s_ref, slice(None), *pack_window(s[:h], s[h : 2 * h], cols // 2), cols // 2)


def factor(s_ref):
    s = unpack_window(s_ref[...].astype(F32))
    half, w = s.shape
    lane = lax.broadcasted_iota(jnp.int32, s.shape, 1)
    return filled(jnp.where(lane >= w - half, s, 0.0)), half


def left_pair(s, half):
    left = left_columns(s, half)
    return left, moved(left, s.shape[1] - half)


def rotor_kernel(n_parts, *refs):
    parts = refs[:n_parts]
    x_ref, s_ref, *a_refs = refs[n_parts:]
    s = cross_of(parts)
    rounded_factor(s_ref, s)
    rotate_into(a_refs, x_ref, *left_pair(low(s).astype(F32), x_ref.shape[1] // 2))


def rotor(parts, x, sizes):
    _, cols = x.shape
    w = window(cols // 2)
    s, *a = pl.pallas_call(
        functools.partial(rotor_kernel, len(parts)),
        in_specs=whole(len(parts) + 1),
        out_specs=whole(1 + len(sizes)),
        out_shape=blocks_of(cols, [cols // 4] + sizes),
        cost_estimate=pl.CostEstimate(flops=4 * sum(sizes) * cols * w, bytes_accessed=6 * sum(sizes) * cols, transcendentals=0),
        compiler_params=params(),
        name="rotor",
    )(*parts, x)
    return s, a


def tail_kernel(s_ref, x_ref, a_ref):
    rotate_into([a_ref], x_ref, *left_pair(*factor(s_ref)), base=x_ref.shape[0] // 2 - a_ref.shape[0])


def tail(s, x, k):
    cols = x.shape[1]
    w = window(cols // 2)
    return pl.pallas_call(
        tail_kernel,
        in_specs=whole(2),
        out_specs=whole(1)[0],
        out_shape=jax.ShapeDtypeStruct((k, cols), BF16),
        cost_estimate=pl.CostEstimate(flops=4 * k * cols * w, bytes_accessed=6 * k * cols, transcendentals=0),
        compiler_params=params(),
        name="tail",
    )(s, x)


def rotate_kernel(s_ref, x_ref, *b_refs):
    s, half = factor(s_ref)
    right = right_columns(s, half)
    rotate_into(b_refs, x_ref, moved(right, half), right)


def rotate(s, x, sizes):
    rows, cols = x.shape
    w = window(cols // 2)
    return pl.pallas_call(
        rotate_kernel,
        in_specs=whole(2),
        out_specs=whole(len(sizes)),
        out_shape=blocks_of(cols, sizes),
        cost_estimate=pl.CostEstimate(flops=2 * rows * cols * w, bytes_accessed=3 * rows * cols, transcendentals=0),
        compiler_params=params(),
        name="rotate",
    )(s, x)


def second_kernel(n_parts, *refs):
    parts = refs[:n_parts]
    s_ref, left_ref = refs[n_parts:]
    s = cross_of(parts)
    rounded_factor(s_ref, s)
    left_ref[...] = left_columns(low(s).astype(F32), s_ref.shape[1] // 2)


def second(parts):
    cols = parts[0].shape[1]
    w = window(cols // 2)
    return pl.pallas_call(
        functools.partial(second_kernel, len(parts)),
        in_specs=whole(len(parts)),
        out_specs=whole(2),
        out_shape=[jax.ShapeDtypeStruct((cols // 4, cols), BF16), jax.ShapeDtypeStruct((cols, w), BF16)],
        cost_estimate=pl.CostEstimate(flops=8 * w**3, bytes_accessed=4 * w * w, transcendentals=0),
        compiler_params=params(),
        name="second",
    )(*parts)


def right_kernel(s_ref, right_ref):
    right_ref[...] = right_columns(*factor(s_ref))


def right_of(s):
    cols = s.shape[1]
    w = window(cols // 2)
    return pl.pallas_call(
        right_kernel,
        in_specs=whole(1),
        out_specs=whole(1)[0],
        out_shape=jax.ShapeDtypeStruct((cols, w), BF16),
        cost_estimate=pl.CostEstimate(flops=8 * w**3, bytes_accessed=4 * w * w, transcendentals=0),
        compiler_params=params(),
        name="right",
    )(s)


def pair_weight(q_ref, first):
    cols, w = q_ref.shape
    half = cols // 2
    rest = jnp.zeros((w - half, w), BF16)
    upper, lower = q_ref[:half], q_ref[half:]
    return jnp.concatenate([upper, rest, lower, rest] if first else [rest, upper, rest, lower], axis=0)


def pair_dot(a_refs, b_refs, start, stop, weight, first):
    w = weight.shape[1]
    cols = a_refs[0].shape[1]
    at = slice(0, w) if first else slice(cols - w, cols)
    a, b = span(a_refs, start, stop)[:, at], span(b_refs, start, stop)[:, at]
    return dot(jnp.concatenate([a, b], axis=1), weight, (1, 0))


def left_kernel(n_a, *refs):
    a_refs, (*b_refs, q_ref, o_ref) = refs[:n_a], refs[n_a:]
    rows = o_ref.shape[0] // 2
    for first in (True, False):
        weight = pair_weight(q_ref, first)
        for start, stop in spans(a_refs, b_refs):
            to = 0 if first else rows
            o_ref[to + start : to + stop, :] = low(pair_dot(a_refs, b_refs, start, stop, weight, first))


def left_half(a, b, q):
    rows, cols = sum(v.shape[0] for v in a), a[0].shape[1]
    w = q.shape[1]
    return pl.pallas_call(
        functools.partial(left_kernel, len(a)),
        in_specs=whole(len(a) + len(b) + 1),
        out_specs=whole(1)[0],
        out_shape=jax.ShapeDtypeStruct((2 * rows, w), BF16),
        cost_estimate=pl.CostEstimate(flops=8 * rows * w * w, bytes_accessed=6 * rows * cols, transcendentals=0),
        compiler_params=params(),
        name="left_half",
    )(*a, *b, q)


def final_kernel(base, cuts, n_a, *refs):
    a_refs, (b_ref, l_ref, q_ref, *_, o_hbm, o_ref, sem) = refs[:n_a], refs[n_a:]
    rows, cols = l_ref.shape[0] // 2, o_ref.shape[1]
    copies = []
    for first in (True, False):
        weight = pair_weight(q_ref, first)
        for start, stop in cuts:
            a, b = span(a_refs, start, stop), b_ref.at[start - base : stop - base]
            right = pair_dot([a], [b], 0, stop - start, weight, first)
            to = slice(start, stop) if first else slice(rows + start, rows + stop)
            shift = -base if first else b_ref.shape[0] - base
            here = slice(start + shift, stop + shift)
            left = l_ref[to, :].astype(F32)
            packed_store(o_ref, here, left, right, cols // 2)
            copy = pltpu.make_async_copy(o_ref.at[here, :], o_hbm.at[to, :], sem.at[len(copies)])
            copy.start()
            copies.append(copy)
    for copy in copies:
        copy.wait()


def final(l, a, b, q):
    rows, cols = l.shape[0], a[0].shape[1]
    w = q.shape[1]
    out, base = [], 0
    for block in b:
        n = block.shape[0]
        cuts = [(i, j) for i, j in spans(a, b) if base <= i < base + n]
        args = (*a, block, l, q, *out)
        out = [
            pl.pallas_call(
                functools.partial(final_kernel, base, cuts, len(a)),
                in_specs=whole(len(a) + 3) + [pl.BlockSpec(memory_space=pltpu.HBM)] * len(out),
                out_specs=pl.BlockSpec(memory_space=pltpu.HBM),
                out_shape=jax.ShapeDtypeStruct((rows, cols), BF16),
                input_output_aliases={len(args) - 1: 0} if out else {},
                scratch_shapes=[pltpu.VMEM((2 * n, cols), BF16), pltpu.SemaphoreType.DMA((2 * len(cuts),))],
                cost_estimate=pl.CostEstimate(flops=8 * n * w * w, bytes_accessed=8 * n * cols, transcendentals=0),
                compiler_params=params(),
                name="final",
            )(*args)
        ]
        base += n
    return out[0]


def passed(x, by):
    n = lax.axis_size("pairs")
    return lax.ppermute(x, "pairs", [(i, (i + 2 * by) % n) for i in range(n)])


def row_parts(g):
    n = lax.axis_size("rows")
    if n & (n - 1) or n > 4:
        return [lax.psum(g.astype(F32), "rows")]
    return [g] + [lax.ppermute(g, "rows", [(i, i ^ k) for i in range(n)]) for k in range(1, n)]


def shares(rows, *parts):
    return [rows * e // 64 for e in parts]


def local(latent):
    rows = latent.shape[0] // 2
    head, middle, last = shares(rows, 36, 8, 20)
    raw_in = passed(taken(latent, last), 1)
    parts = row_parts(gram(latent, 4))
    s, a = rotor(parts, latent, [head, middle])
    s_in = passed(s, 1)
    a_in = [passed(a[0], 1)]
    a_in.append(passed(a[1], 1))
    b = rotate(s, latent, shares(rows, 44, 20))
    a.append(tail(s, latent, last))
    a_in.append(tail(s_in, raw_in, last))
    a_in[0], b_out = lax.optimization_barrier((a_in[0], b[0]))
    b_in = [passed(b_out, -1)]
    s, left = second(row_parts(gram_pair(a_in, b)))
    s_in = passed(s, -1)
    left, b_out = lax.optimization_barrier((left, b[1]))
    b_in.append(passed(b_out, -1))
    return final(left_half(a_in, b, left), a, b_in, right_of(s_in))


def solution(mesh):
    return jax.shard_map(
        local,
        mesh=mesh,
        in_specs=(P("rows", "pairs"),),
        out_specs=P("rows", "pairs"),
        check_vma=False,
    )
```

```python
import functools
import math

import jax
import jax.numpy as jnp
import numpy as np
from jax import lax
from jax.experimental import pallas as pl
from jax.experimental.pallas import tpu as pltpu
from jax.sharding import PartitionSpec as P


F32, BF16 = jnp.float32, jnp.bfloat16
LANES = 128


def polar_coefficients():
    c = 1.5 / math.sqrt(65.0)
    mul, sub = np.polynomial.polynomial.polymul, np.polynomial.polynomial.polysub
    n = np.array([c * c, c * c])
    u = np.array([1.5 - 0.5 * c * c, -0.5 * c * c])
    return [float(v) for v in c * sub(1.5 * u, 0.5 * mul(n, mul(u, mul(u, u))))]


COEF = polar_coefficients()


def window(half):
    return -(-half // LANES) * LANES


def dot(a, b, contract):
    return lax.dot_general(a, b, ((contract[:1], contract[1:]), ((), ())), preferred_element_type=F32)


def low(a):
    return a.astype(BF16)


def params():
    return pltpu.CompilerParams(vmem_limit_bytes=16 << 20)


def whole(n):
    return [pl.BlockSpec(memory_space=pltpu.VMEM)] * n


def pieces(rows, n):
    return [slice(i * (rows // n), (i + 1) * (rows // n)) for i in range(n)]


def spans(*lists):
    cuts = {0}
    for blocks in lists:
        stop = 0
        for block in blocks:
            stop += block.shape[0]
            cuts.add(stop)
    cuts = sorted(cuts)
    return list(zip(cuts[:-1], cuts[1:]))


def span(blocks, start, stop):
    for block in blocks:
        if start < block.shape[0]:
            return block.at[start:stop]
        start, stop = start - block.shape[0], stop - block.shape[0]


def blocks_of(cols, sizes):
    return [jax.ShapeDtypeStruct((n, cols), BF16) for n in sizes]


def pack_window(top, bot, half):
    w = top.shape[1]
    lane = lax.broadcasted_iota(jnp.int32, top.shape, 1)
    return jnp.where(lane < half, pltpu.roll(top, half, 1), 0.0), jnp.where(lane >= w - half, bot, 0.0)


def unpack_window(packed):
    cols = packed.shape[1]
    half = cols // 2
    w = window(half)
    return jnp.concatenate([pltpu.roll(packed[:, :w], w - half, 1), packed[:, cols - w :]], axis=0)


def pack_stats(g_ref, cross, norms):
    half, _ = cross.shape
    h = half // 2
    packed_store(g_ref, slice(0, h), *pack_window(cross[:h], cross[h:], half), half)
    row = lax.broadcasted_iota(jnp.int32, (8, g_ref.shape[1]), 0)
    g_ref[h:] = low(jnp.where(row == 0, norms, 0.0))


def stats_shape(cols):
    return jax.ShapeDtypeStruct((cols // 4 + 8, cols), BF16)


def taken_kernel(x_hbm, raw_ref, sem):
    rows, k = x_hbm.shape[0], raw_ref.shape[0] // 2
    copies = [
        pltpu.make_async_copy(x_hbm.at[stop - k : stop, :], raw_ref.at[i * k : (i + 1) * k, :], sem.at[i])
        for i, stop in enumerate((rows // 2, rows))
    ]
    for copy in copies:
        copy.start()
    for copy in copies:
        copy.wait()


def taken(x, k):
    cols = x.shape[1]
    return pl.pallas_call(
        taken_kernel,
        in_specs=[pl.BlockSpec(memory_space=pltpu.HBM)],
        out_specs=whole(1)[0],
        out_shape=jax.ShapeDtypeStruct((2 * k, cols), BF16),
        scratch_shapes=[pltpu.SemaphoreType.DMA((2,))],
        cost_estimate=pl.CostEstimate(flops=0, bytes_accessed=8 * k * cols, transcendentals=0),
        compiler_params=params(),
        name="taken",
    )(pltpu.with_memory_space_constraint(x, pltpu.HBM))


def gram_kernel(n, x_ref, g_ref):
    rows, cols = x_ref.shape
    half = cols // 2
    w = window(half)
    cross, norms = jnp.zeros((w, w), F32), jnp.zeros((1, cols), F32)
    for r in pieces(rows, n):
        x = x_ref[r, :]
        cross += dot(x[:, :w], x[:, cols - w :], (0, 0))
        xf = x.astype(F32)
        norms += jnp.sum(xf * xf, axis=0, keepdims=True)
    pack_stats(g_ref, cross[:half], norms)


def gram(x, n):
    rows, cols = x.shape
    w = window(cols // 2)
    return pl.pallas_call(
        functools.partial(gram_kernel, n),
        in_specs=whole(1),
        out_specs=whole(1)[0],
        out_shape=stats_shape(cols),
        cost_estimate=pl.CostEstimate(flops=2 * rows * w * w, bytes_accessed=2 * rows * cols, transcendentals=0),
        compiler_params=params(),
        name="gram",
    )(x)


def gram_pair_kernel(n_a, *refs):
    a_refs, b_refs, g_ref = refs[:n_a], refs[n_a:-1], refs[-1]
    cols = g_ref.shape[1]
    half = cols // 2
    w = window(half)
    pad, o = w - half, cols - w
    top, bot = jnp.zeros((w, w), F32), jnp.zeros((w, w), F32)
    norm_a, norm_b = jnp.zeros((1, cols), F32), jnp.zeros((1, cols), F32)
    for start, stop in spans(a_refs, b_refs):
        a, b = span(a_refs, start, stop)[...], span(b_refs, start, stop)[...]
        top += dot(a[:, :w], b[:, :w], (0, 0))
        bot += dot(a[:, o:], b[:, o:], (0, 0))
        af, bf = a.astype(F32), b.astype(F32)
        norm_a += jnp.sum(af * af, axis=0, keepdims=True)
        norm_b += jnp.sum(bf * bf, axis=0, keepdims=True)
    cross = pltpu.roll(top[:half], pad, 1) + bot[pad:]
    s, t = jnp.broadcast_to(norm_a, (8, cols)), jnp.broadcast_to(norm_b, (8, cols))
    left = s + jnp.concatenate([pltpu.roll(s[:, o:], half, 1), jnp.zeros((8, o), F32)], axis=1)
    right = t + jnp.concatenate([jnp.zeros((8, o), F32), pltpu.roll(t[:, :w], pad, 1)], axis=1)
    lane = lax.broadcasted_iota(jnp.int32, (8, cols), 1)
    pack_stats(g_ref, cross, jnp.where(lane < half, left, right)[:1])


def gram_pair(a, b):
    cols = a[0].shape[1]
    rows = sum(v.shape[0] for v in a)
    w = window(cols // 2)
    return pl.pallas_call(
        functools.partial(gram_pair_kernel, len(a)),
        in_specs=whole(len(a) + len(b)),
        out_specs=whole(1)[0],
        out_shape=stats_shape(cols),
        cost_estimate=pl.CostEstimate(flops=4 * rows * w * w, bytes_accessed=4 * rows * cols, transcendentals=0),
        compiler_params=params(),
        name="gram_pair",
    )(*a, *b)


def cross_of(parts):
    total = sum((p[...].astype(F32) for p in parts[1:]), parts[0][...].astype(F32))
    cols = total.shape[1]
    half = cols // 2
    w = window(half)
    pad, h = w - half, half // 2
    cross = unpack_window(total[:h])
    norms = total[h:]
    left = jnp.transpose(norms[:, :w])[:half, :1]
    corr = cross * (lax.rsqrt(left) * lax.rsqrt(norms[:1, cols - w :]))
    lane = lax.broadcasted_iota(jnp.int32, corr.shape, 1)
    corr = jnp.where(lane >= pad, corr, 0.0)
    size = jnp.sqrt(2.0 * jnp.sum(corr * corr) + 1e-12)
    return filled(corr * (8.0 / size))


def filled(x):
    half, w = x.shape
    return jnp.concatenate([x, jnp.zeros((w - half, w), F32)], axis=0) if w > half else x


def minus_constant(k, k2):
    return COEF[1] * k + COEF[2] * k2 + dot(low(k2), low(COEF[3] * k + COEF[4] * k2), (1, 0))


def eye_at(w, first, stop):
    r = lax.broadcasted_iota(jnp.int32, (w, w), 0)
    c = lax.broadcasted_iota(jnp.int32, (w, w), 1)
    return (r == c) & (r >= first) & (r < stop)


def left_columns(x, half):
    w = x.shape[1]
    xb = low(x)
    k = dot(xb, xb, (1, 1))
    delta = minus_constant(k, dot(low(k), low(k), (1, 0)))
    upper = delta + jnp.where(eye_at(w, 0, half), COEF[0], 0.0)
    lower = -(COEF[0] * jnp.transpose(x) + dot(xb, low(delta), (0, 0)))
    return low(jnp.concatenate([upper[:half], lower[w - half :]], axis=0))


def right_columns(x, half):
    w = x.shape[1]
    xb = low(x)
    k = dot(xb, xb, (0, 0))
    delta = minus_constant(k, dot(low(k), low(k), (1, 0)))
    upper = COEF[0] * x + dot(xb, low(delta), (1, 0))
    lower = delta + jnp.where(eye_at(w, w - half, w), COEF[0], 0.0)
    return low(jnp.concatenate([upper[:half], lower[w - half :]], axis=0))


def moved(q, by):
    return low(pltpu.roll(q.astype(F32), by, 1)) if by else q


def packed_store(ref, rows, top, bot, half):
    w = top.shape[1]
    o = 2 * half - w
    ref[rows, :o] = low(top[:, :o])
    if w > o:
        ref[rows, o:w] = low(top[:, o:] + bot[:, : w - o])
    ref[rows, w:] = low(bot[:, w - o :])


def rotate_into(refs, x_ref, q_top, q_bot, base=0):
    rows, half = x_ref.shape[0] // 2, x_ref.shape[1] // 2
    for start, stop in spans(refs):
        top = dot(x_ref[base + start : base + stop, :], q_top, (1, 0))
        bot = dot(x_ref[rows + base + start : rows + base + stop, :], q_bot, (1, 0))
        packed_store(span(refs, start, stop), slice(None), top, bot, half)


def rounded_factor(s_ref, s):
    h, cols = s_ref.shape
    packed_store(s_ref, slice(None), *pack_window(s[:h], s[h : 2 * h], cols // 2), cols // 2)


def own_share(s_ref, n):
    s = s_ref[...].astype(F32)
    h = s.shape[0] // n
    me, share = lax.axis_index("rows"), s[:h]
    for k in range(1, n):
        share = jnp.where(me == k, s[k * h : (k + 1) * h], share)
    return low(share)


def joined(share_refs):
    shares = [ref[...].astype(F32) for ref in share_refs]
    if len(shares) == 1:
        return shares[0]
    me, rows = lax.axis_index("rows"), []
    for at in range(len(shares)):
        row = shares[0]
        for k in range(1, len(shares)):
            row = jnp.where(me == at ^ k, shares[k], row)
        rows.append(row)
    return jnp.concatenate(rows, axis=0)


def shared(cols):
    n = lax.axis_size("rows")
    return n if n <= 4 and not n & (n - 1) and (cols // 4) % (8 * n) == 0 else 1


def factor(*share_refs):
    s = unpack_window(joined(share_refs))
    half, w = s.shape
    lane = lax.broadcasted_iota(jnp.int32, s.shape, 1)
    return filled(jnp.where(lane >= w - half, s, 0.0)), half


def left_pair(s, half):
    left = left_columns(s, half)
    return left, moved(left, s.shape[1] - half)


def rotor_kernel(n_parts, *refs):
    parts = refs[:n_parts]
    x_ref, s_ref, share_ref, *a_refs = refs[n_parts:]
    s = cross_of(parts)
    rounded_factor(s_ref, s)
    share_ref[...] = own_share(s_ref, s_ref.shape[0] // share_ref.shape[0])
    rotate_into(a_refs, x_ref, *left_pair(low(s).astype(F32), x_ref.shape[1] // 2))


def rotor(parts, x, sizes):
    _, cols = x.shape
    w = window(cols // 2)
    s, share, *a = pl.pallas_call(
        functools.partial(rotor_kernel, len(parts)),
        in_specs=whole(len(parts) + 1),
        out_specs=whole(2 + len(sizes)),
        out_shape=blocks_of(cols, [cols // 4, cols // 4 // shared(cols)] + sizes),
        cost_estimate=pl.CostEstimate(flops=4 * sum(sizes) * cols * w, bytes_accessed=6 * sum(sizes) * cols, transcendentals=0),
        compiler_params=params(),
        name="rotor",
    )(*parts, x)
    return s, share, a


def tail_kernel(*refs):
    *s_refs, x_ref, a_ref = refs
    rotate_into([a_ref], x_ref, *left_pair(*factor(*s_refs)), base=x_ref.shape[0] // 2 - a_ref.shape[0])


def tail(s, x, k):
    cols = x.shape[1]
    w = window(cols // 2)
    return pl.pallas_call(
        tail_kernel,
        in_specs=whole(len(s) + 1),
        out_specs=whole(1)[0],
        out_shape=jax.ShapeDtypeStruct((k, cols), BF16),
        cost_estimate=pl.CostEstimate(flops=4 * k * cols * w, bytes_accessed=6 * k * cols, transcendentals=0),
        compiler_params=params(),
        name="tail",
    )(*s, x)


def rotate_kernel(s_ref, x_ref, *b_refs):
    s, half = factor(s_ref)
    right = right_columns(s, half)
    rotate_into(b_refs, x_ref, moved(right, half), right)


def rotate(s, x, sizes):
    rows, cols = x.shape
    w = window(cols // 2)
    return pl.pallas_call(
        rotate_kernel,
        in_specs=whole(2),
        out_specs=whole(len(sizes)),
        out_shape=blocks_of(cols, sizes),
        cost_estimate=pl.CostEstimate(flops=2 * rows * cols * w, bytes_accessed=3 * rows * cols, transcendentals=0),
        compiler_params=params(),
        name="rotate",
    )(s, x)


def second_kernel(n_parts, *refs):
    parts = refs[:n_parts]
    s_ref, left_ref = refs[n_parts:]
    s = cross_of(parts)
    rounded_factor(s_ref, s)
    left_ref[...] = left_columns(low(s).astype(F32), s_ref.shape[1] // 2)


def second(parts):
    cols = parts[0].shape[1]
    w = window(cols // 2)
    return pl.pallas_call(
        functools.partial(second_kernel, len(parts)),
        in_specs=whole(len(parts)),
        out_specs=whole(2),
        out_shape=[jax.ShapeDtypeStruct((cols // 4, cols), BF16), jax.ShapeDtypeStruct((cols, w), BF16)],
        cost_estimate=pl.CostEstimate(flops=8 * w**3, bytes_accessed=4 * w * w, transcendentals=0),
        compiler_params=params(),
        name="second",
    )(*parts)


def right_kernel(s_ref, right_ref):
    right_ref[...] = right_columns(*factor(s_ref))


def right_of(s):
    cols = s.shape[1]
    w = window(cols // 2)
    return pl.pallas_call(
        right_kernel,
        in_specs=whole(1),
        out_specs=whole(1)[0],
        out_shape=jax.ShapeDtypeStruct((cols, w), BF16),
        cost_estimate=pl.CostEstimate(flops=8 * w**3, bytes_accessed=4 * w * w, transcendentals=0),
        compiler_params=params(),
        name="right",
    )(s)


def pair_weight(q_ref, first):
    cols, w = q_ref.shape
    half = cols // 2
    rest = jnp.zeros((w - half, w), BF16)
    upper, lower = q_ref[:half], q_ref[half:]
    return jnp.concatenate([upper, rest, lower, rest] if first else [rest, upper, rest, lower], axis=0)


def pair_dot(a_refs, b_refs, start, stop, weight, first):
    w = weight.shape[1]
    cols = a_refs[0].shape[1]
    at = slice(0, w) if first else slice(cols - w, cols)
    a, b = span(a_refs, start, stop)[:, at], span(b_refs, start, stop)[:, at]
    return dot(jnp.concatenate([a, b], axis=1), weight, (1, 0))


def left_kernel(n_a, *refs):
    a_refs, (*b_refs, q_ref, o_ref) = refs[:n_a], refs[n_a:]
    rows = o_ref.shape[0] // 2
    for first in (True, False):
        weight = pair_weight(q_ref, first)
        for start, stop in spans(a_refs, b_refs):
            to = 0 if first else rows
            o_ref[to + start : to + stop, :] = low(pair_dot(a_refs, b_refs, start, stop, weight, first))


def left_half(a, b, q):
    rows, cols = sum(v.shape[0] for v in a), a[0].shape[1]
    w = q.shape[1]
    return pl.pallas_call(
        functools.partial(left_kernel, len(a)),
        in_specs=whole(len(a) + len(b) + 1),
        out_specs=whole(1)[0],
        out_shape=jax.ShapeDtypeStruct((2 * rows, w), BF16),
        cost_estimate=pl.CostEstimate(flops=8 * rows * w * w, bytes_accessed=6 * rows * cols, transcendentals=0),
        compiler_params=params(),
        name="left_half",
    )(*a, *b, q)


def final_kernel(base, cuts, n_a, *refs):
    a_refs, (b_ref, l_ref, q_ref, *_, o_hbm, o_ref, sem) = refs[:n_a], refs[n_a:]
    rows, cols = l_ref.shape[0] // 2, o_ref.shape[1]
    copies = []
    for first in (True, False):
        weight = pair_weight(q_ref, first)
        for start, stop in cuts:
            a, b = span(a_refs, start, stop), b_ref.at[start - base : stop - base]
            right = pair_dot([a], [b], 0, stop - start, weight, first)
            to = slice(start, stop) if first else slice(rows + start, rows + stop)
            shift = -base if first else b_ref.shape[0] - base
            here = slice(start + shift, stop + shift)
            left = l_ref[to, :].astype(F32)
            packed_store(o_ref, here, left, right, cols // 2)
            copy = pltpu.make_async_copy(o_ref.at[here, :], o_hbm.at[to, :], sem.at[len(copies)])
            copy.start()
            copies.append(copy)
    for copy in copies:
        copy.wait()


def final(l, a, b, q):
    rows, cols = l.shape[0], a[0].shape[1]
    w = q.shape[1]
    out, base = [], 0
    for block in b:
        n = block.shape[0]
        cuts = [(i, j) for i, j in spans(a, b) if base <= i < base + n]
        args = (*a, block, l, q, *out)
        out = [
            pl.pallas_call(
                functools.partial(final_kernel, base, cuts, len(a)),
                in_specs=whole(len(a) + 3) + [pl.BlockSpec(memory_space=pltpu.HBM)] * len(out),
                out_specs=pl.BlockSpec(memory_space=pltpu.HBM),
                out_shape=jax.ShapeDtypeStruct((rows, cols), BF16),
                input_output_aliases={len(args) - 1: 0} if out else {},
                scratch_shapes=[pltpu.VMEM((2 * n, cols), BF16), pltpu.SemaphoreType.DMA((2 * len(cuts),))],
                cost_estimate=pl.CostEstimate(flops=8 * n * w * w, bytes_accessed=8 * n * cols, transcendentals=0),
                compiler_params=params(),
                name="final",
            )(*args)
        ]
        base += n
    return out[0]


def passed(x, by):
    n = lax.axis_size("pairs")
    return lax.ppermute(x, "pairs", [(i, (i + 2 * by) % n) for i in range(n)])


def row_parts(g):
    n = lax.axis_size("rows")
    if n & (n - 1) or n > 4:
        return [lax.psum(g.astype(F32), "rows")]
    return [g] + [lax.ppermute(g, "rows", [(i, i ^ k) for i in range(n)]) for k in range(1, n)]


def shares(rows, *parts):
    return [rows * e // 64 for e in parts]


def local(latent):
    rows = latent.shape[0] // 2
    head, middle, last = shares(rows, 34, 8, 22)
    raw_in = passed(taken(latent, last), 1)
    parts = row_parts(gram(latent, 4))
    s, share, a = rotor(parts, latent, [head, middle])
    share_in = passed(share, 1)
    a_in = [passed(a[0], 1)]
    a_in.append(passed(a[1], 1))
    b = rotate(s, latent, shares(rows, 44, 20))
    a.append(tail([s], latent, last))
    s_in = row_parts(share_in) if shared(latent.shape[1]) > 1 else [share_in]
    a_in.append(tail(s_in, raw_in, last))
    a_in[0], b_out = lax.optimization_barrier((a_in[0], b[0]))
    b_in = [passed(b_out, -1)]
    s, left = second(row_parts(gram_pair(a_in, b)))
    s_in = passed(s, -1)
    left, b_out = lax.optimization_barrier((left, b[1]))
    b_in.append(passed(b_out, -1))
    return final(left_half(a_in, b, left), a, b_in, right_of(s_in))


def solution(mesh):
    return jax.shard_map(
        local,
        mesh=mesh,
        in_specs=(P("rows", "pairs"),),
        out_specs=P("rows", "pairs"),
        check_vma=False,
    )
```

```python
import functools
import math

import jax
import jax.numpy as jnp
import numpy as np
from jax import lax
from jax.experimental import pallas as pl
from jax.experimental.pallas import tpu as pltpu
from jax.sharding import PartitionSpec as P


F32, BF16 = jnp.float32, jnp.bfloat16
LANES = 128


def polar_coefficients():
    c = 1.5 / math.sqrt(65.0)
    mul, sub = np.polynomial.polynomial.polymul, np.polynomial.polynomial.polysub
    n = np.array([c * c, c * c])
    u = np.array([1.5 - 0.5 * c * c, -0.5 * c * c])
    return [float(v) for v in c * sub(1.5 * u, 0.5 * mul(n, mul(u, mul(u, u))))]


COEF = polar_coefficients()


def window(half):
    return -(-half // LANES) * LANES


def dot(a, b, contract):
    return lax.dot_general(a, b, ((contract[:1], contract[1:]), ((), ())), preferred_element_type=F32)


def low(a):
    return a.astype(BF16)


def params():
    return pltpu.CompilerParams(vmem_limit_bytes=16 << 20)


def whole(n):
    return [pl.BlockSpec(memory_space=pltpu.VMEM)] * n


def pieces(rows, n):
    return [slice(i * (rows // n), (i + 1) * (rows // n)) for i in range(n)]


def spans(*lists):
    cuts = {0}
    for blocks in lists:
        stop = 0
        for block in blocks:
            stop += block.shape[0]
            cuts.add(stop)
    cuts = sorted(cuts)
    return list(zip(cuts[:-1], cuts[1:]))


def span(blocks, start, stop):
    for block in blocks:
        if start < block.shape[0]:
            return block.at[start:stop]
        start, stop = start - block.shape[0], stop - block.shape[0]


def blocks_of(cols, sizes):
    return [jax.ShapeDtypeStruct((n, cols), BF16) for n in sizes]


def pack_window(top, bot, half):
    w = top.shape[1]
    lane = lax.broadcasted_iota(jnp.int32, top.shape, 1)
    return jnp.where(lane < half, pltpu.roll(top, half, 1), 0.0), jnp.where(lane >= w - half, bot, 0.0)


def unpack_window(packed):
    cols = packed.shape[1]
    half = cols // 2
    w = window(half)
    return jnp.concatenate([pltpu.roll(packed[:, :w], w - half, 1), packed[:, cols - w :]], axis=0)


def pack_stats(g_ref, cross, norms):
    half, _ = cross.shape
    h = half // 2
    packed_store(g_ref, slice(0, h), *pack_window(cross[:h], cross[h:], half), half)
    row = lax.broadcasted_iota(jnp.int32, (8, g_ref.shape[1]), 0)
    rest = norms - low(norms).astype(F32)
    g_ref[h:] = low(jnp.where(row == 0, norms, jnp.where(row == 1, rest, 0.0)))


def stats_shape(cols):
    return jax.ShapeDtypeStruct((cols // 4 + 8, cols), BF16)


def taken_kernel(x_hbm, raw_ref, sem):
    rows, k = x_hbm.shape[0], raw_ref.shape[0] // 2
    copies = [
        pltpu.make_async_copy(x_hbm.at[stop - k : stop, :], raw_ref.at[i * k : (i + 1) * k, :], sem.at[i])
        for i, stop in enumerate((rows // 2, rows))
    ]
    for copy in copies:
        copy.start()
    for copy in copies:
        copy.wait()


def taken(x, k):
    cols = x.shape[1]
    return pl.pallas_call(
        taken_kernel,
        in_specs=[pl.BlockSpec(memory_space=pltpu.HBM)],
        out_specs=whole(1)[0],
        out_shape=jax.ShapeDtypeStruct((2 * k, cols), BF16),
        scratch_shapes=[pltpu.SemaphoreType.DMA((2,))],
        cost_estimate=pl.CostEstimate(flops=0, bytes_accessed=8 * k * cols, transcendentals=0),
        compiler_params=params(),
        name="taken",
    )(pltpu.with_memory_space_constraint(x, pltpu.HBM))


def gram_kernel(n, x_ref, g_ref):
    rows, cols = x_ref.shape
    half = cols // 2
    w = window(half)
    cross, norms = jnp.zeros((w, w), F32), jnp.zeros((1, cols), F32)
    for r in pieces(rows, n):
        x = x_ref[r, :]
        cross += dot(x[:, :w], x[:, cols - w :], (0, 0))
        xf = x.astype(F32)
        norms += jnp.sum(xf * xf, axis=0, keepdims=True)
    pack_stats(g_ref, cross[:half], norms)


def gram(x, n):
    rows, cols = x.shape
    w = window(cols // 2)
    return pl.pallas_call(
        functools.partial(gram_kernel, n),
        in_specs=whole(1),
        out_specs=whole(1)[0],
        out_shape=stats_shape(cols),
        cost_estimate=pl.CostEstimate(flops=2 * rows * w * w, bytes_accessed=2 * rows * cols, transcendentals=0),
        compiler_params=params(),
        name="gram",
    )(x)


def gram_pair_kernel(n_a, *refs):
    a_refs, b_refs, g_ref = refs[:n_a], refs[n_a:-1], refs[-1]
    cols = g_ref.shape[1]
    half = cols // 2
    w = window(half)
    pad, o = w - half, cols - w
    top, bot = jnp.zeros((w, w), F32), jnp.zeros((w, w), F32)
    norm_a, norm_b = jnp.zeros((1, cols), F32), jnp.zeros((1, cols), F32)
    for start, stop in spans(a_refs, b_refs):
        a, b = span(a_refs, start, stop)[...], span(b_refs, start, stop)[...]
        top += dot(a[:, :w], b[:, :w], (0, 0))
        bot += dot(a[:, o:], b[:, o:], (0, 0))
        af, bf = a.astype(F32), b.astype(F32)
        norm_a += jnp.sum(af * af, axis=0, keepdims=True)
        norm_b += jnp.sum(bf * bf, axis=0, keepdims=True)
    cross = pltpu.roll(top[:half], pad, 1) + bot[pad:]
    s, t = jnp.broadcast_to(norm_a, (8, cols)), jnp.broadcast_to(norm_b, (8, cols))
    left = s + jnp.concatenate([pltpu.roll(s[:, o:], half, 1), jnp.zeros((8, o), F32)], axis=1)
    right = t + jnp.concatenate([jnp.zeros((8, o), F32), pltpu.roll(t[:, :w], pad, 1)], axis=1)
    lane = lax.broadcasted_iota(jnp.int32, (8, cols), 1)
    pack_stats(g_ref, cross, jnp.where(lane < half, left, right)[:1])


def gram_pair(a, b):
    cols = a[0].shape[1]
    rows = sum(v.shape[0] for v in a)
    w = window(cols // 2)
    return pl.pallas_call(
        functools.partial(gram_pair_kernel, len(a)),
        in_specs=whole(len(a) + len(b)),
        out_specs=whole(1)[0],
        out_shape=stats_shape(cols),
        cost_estimate=pl.CostEstimate(flops=4 * rows * w * w, bytes_accessed=4 * rows * cols, transcendentals=0),
        compiler_params=params(),
        name="gram_pair",
    )(*a, *b)


def cross_of(parts):
    total = sum((p[...].astype(F32) for p in parts[1:]), parts[0][...].astype(F32))
    cols = total.shape[1]
    half = cols // 2
    w = window(half)
    pad, h = w - half, half // 2
    cross = unpack_window(total[:h])
    norms = total[h:] + pltpu.roll(total[h:], 7, 0)
    left = jnp.transpose(norms[:, :w])[:half, :1]
    corr = cross * (lax.rsqrt(left) * lax.rsqrt(norms[:1, cols - w :]))
    lane = lax.broadcasted_iota(jnp.int32, corr.shape, 1)
    corr = jnp.where(lane >= pad, corr, 0.0)
    size = jnp.sqrt(2.0 * jnp.sum(corr * corr) + 1e-12)
    return filled(corr * (8.0 / size))


def filled(x):
    half, w = x.shape
    return jnp.concatenate([x, jnp.zeros((w - half, w), F32)], axis=0) if w > half else x


def split(a):
    high = low(a)
    return high, low(a - high.astype(F32))


def split_dot(a, b, contract=(1, 0)):
    return dot(a[0], b[0], contract) + (dot(a[0], b[1], contract) + dot(a[1], b[0], contract))


def minus_constant(k):
    words = split(k)
    k2 = split_dot(words, words)
    return COEF[1] * k + COEF[2] * k2 + split_dot(split(k2), split(COEF[3] * k + COEF[4] * k2))


def word_dot(x, delta, contract):
    high, rest = split(delta)
    return dot(x, high, contract) + dot(x, rest, contract)


def eye_at(w, first, stop):
    r = lax.broadcasted_iota(jnp.int32, (w, w), 0)
    c = lax.broadcasted_iota(jnp.int32, (w, w), 1)
    return (r == c) & (r >= first) & (r < stop)


def left_columns(x, half):
    w = x.shape[1]
    xb = low(x)
    k = dot(xb, xb, (1, 1))
    delta = minus_constant(k)
    upper = delta + jnp.where(eye_at(w, 0, half), COEF[0], 0.0)
    lower = -(COEF[0] * jnp.transpose(x) + word_dot(xb, delta, (0, 0)))
    return low(jnp.concatenate([upper[:half], lower[w - half :]], axis=0))


def right_columns(x, half):
    w = x.shape[1]
    xb = low(x)
    k = dot(xb, xb, (0, 0))
    delta = minus_constant(k)
    upper = COEF[0] * x + word_dot(xb, delta, (1, 0))
    lower = delta + jnp.where(eye_at(w, w - half, w), COEF[0], 0.0)
    return low(jnp.concatenate([upper[:half], lower[w - half :]], axis=0))


def moved(q, by):
    return low(pltpu.roll(q.astype(F32), by, 1)) if by else q


def packed_store(ref, rows, top, bot, half):
    w = top.shape[1]
    o = 2 * half - w
    ref[rows, :o] = low(top[:, :o])
    if w > o:
        ref[rows, o:w] = low(top[:, o:] + bot[:, : w - o])
    ref[rows, w:] = low(bot[:, w - o :])


def rotate_into(refs, x_ref, q_top, q_bot, base=0):
    rows, half = x_ref.shape[0] // 2, x_ref.shape[1] // 2
    for start, stop in spans(refs):
        top = dot(x_ref[base + start : base + stop, :], q_top, (1, 0))
        bot = dot(x_ref[rows + base + start : rows + base + stop, :], q_bot, (1, 0))
        packed_store(span(refs, start, stop), slice(None), top, bot, half)


def rounded_factor(s_ref, s):
    h, cols = s_ref.shape
    packed_store(s_ref, slice(None), *pack_window(s[:h], s[h : 2 * h], cols // 2), cols // 2)


def own_share(s_ref, n):
    s = s_ref[...].astype(F32)
    h = s.shape[0] // n
    me, share = lax.axis_index("rows"), s[:h]
    for k in range(1, n):
        share = jnp.where(me == k, s[k * h : (k + 1) * h], share)
    return low(share)


def joined(share_refs):
    shares = [ref[...].astype(F32) for ref in share_refs]
    if len(shares) == 1:
        return shares[0]
    me, rows = lax.axis_index("rows"), []
    for at in range(len(shares)):
        row = shares[0]
        for k in range(1, len(shares)):
            row = jnp.where(me == at ^ k, shares[k], row)
        rows.append(row)
    return jnp.concatenate(rows, axis=0)


def shared(cols):
    n = lax.axis_size("rows")
    return n if n <= 4 and not n & (n - 1) and (cols // 4) % (8 * n) == 0 else 1


def factor(*share_refs):
    s = unpack_window(joined(share_refs))
    half, w = s.shape
    lane = lax.broadcasted_iota(jnp.int32, s.shape, 1)
    return filled(jnp.where(lane >= w - half, s, 0.0)), half


def left_pair(s, half):
    left = left_columns(s, half)
    return left, moved(left, s.shape[1] - half)


def rotor_kernel(n_parts, *refs):
    parts = refs[:n_parts]
    x_ref, s_ref, share_ref, *a_refs = refs[n_parts:]
    s = cross_of(parts)
    rounded_factor(s_ref, s)
    share_ref[...] = own_share(s_ref, s_ref.shape[0] // share_ref.shape[0])
    rotate_into(a_refs, x_ref, *left_pair(low(s).astype(F32), x_ref.shape[1] // 2))


def rotor(parts, x, sizes):
    _, cols = x.shape
    w = window(cols // 2)
    s, share, *a = pl.pallas_call(
        functools.partial(rotor_kernel, len(parts)),
        in_specs=whole(len(parts) + 1),
        out_specs=whole(2 + len(sizes)),
        out_shape=blocks_of(cols, [cols // 4, cols // 4 // shared(cols)] + sizes),
        cost_estimate=pl.CostEstimate(flops=4 * sum(sizes) * cols * w, bytes_accessed=6 * sum(sizes) * cols, transcendentals=0),
        compiler_params=params(),
        name="rotor",
    )(*parts, x)
    return s, share, a


def tail_kernel(*refs):
    *s_refs, x_ref, a_ref = refs
    rotate_into([a_ref], x_ref, *left_pair(*factor(*s_refs)), base=x_ref.shape[0] // 2 - a_ref.shape[0])


def tail(s, x, k):
    cols = x.shape[1]
    w = window(cols // 2)
    return pl.pallas_call(
        tail_kernel,
        in_specs=whole(len(s) + 1),
        out_specs=whole(1)[0],
        out_shape=jax.ShapeDtypeStruct((k, cols), BF16),
        cost_estimate=pl.CostEstimate(flops=4 * k * cols * w, bytes_accessed=6 * k * cols, transcendentals=0),
        compiler_params=params(),
        name="tail",
    )(*s, x)


def rotate_kernel(s_ref, x_ref, *b_refs):
    s, half = factor(s_ref)
    right = right_columns(s, half)
    rotate_into(b_refs, x_ref, moved(right, half), right)


def rotate(s, x, sizes):
    rows, cols = x.shape
    w = window(cols // 2)
    return pl.pallas_call(
        rotate_kernel,
        in_specs=whole(2),
        out_specs=whole(len(sizes)),
        out_shape=blocks_of(cols, sizes),
        cost_estimate=pl.CostEstimate(flops=2 * rows * cols * w, bytes_accessed=3 * rows * cols, transcendentals=0),
        compiler_params=params(),
        name="rotate",
    )(s, x)


def second_kernel(n_parts, *refs):
    parts = refs[:n_parts]
    s_ref, left_ref = refs[n_parts:]
    s = cross_of(parts)
    rounded_factor(s_ref, s)
    left_ref[...] = left_columns(low(s).astype(F32), s_ref.shape[1] // 2)


def second(parts):
    cols = parts[0].shape[1]
    w = window(cols // 2)
    return pl.pallas_call(
        functools.partial(second_kernel, len(parts)),
        in_specs=whole(len(parts)),
        out_specs=whole(2),
        out_shape=[jax.ShapeDtypeStruct((cols // 4, cols), BF16), jax.ShapeDtypeStruct((cols, w), BF16)],
        cost_estimate=pl.CostEstimate(flops=8 * w**3, bytes_accessed=4 * w * w, transcendentals=0),
        compiler_params=params(),
        name="second",
    )(*parts)


def right_kernel(s_ref, right_ref):
    right_ref[...] = right_columns(*factor(s_ref))


def right_of(s):
    cols = s.shape[1]
    w = window(cols // 2)
    return pl.pallas_call(
        right_kernel,
        in_specs=whole(1),
        out_specs=whole(1)[0],
        out_shape=jax.ShapeDtypeStruct((cols, w), BF16),
        cost_estimate=pl.CostEstimate(flops=8 * w**3, bytes_accessed=4 * w * w, transcendentals=0),
        compiler_params=params(),
        name="right",
    )(s)


def pair_weight(q_ref, first):
    cols, w = q_ref.shape
    half = cols // 2
    rest = jnp.zeros((w - half, w), BF16)
    upper, lower = q_ref[:half], q_ref[half:]
    return jnp.concatenate([upper, rest, lower, rest] if first else [rest, upper, rest, lower], axis=0)


def pair_dot(a_refs, b_refs, start, stop, weight, first):
    w = weight.shape[1]
    cols = a_refs[0].shape[1]
    at = slice(0, w) if first else slice(cols - w, cols)
    a, b = span(a_refs, start, stop)[:, at], span(b_refs, start, stop)[:, at]
    return dot(jnp.concatenate([a, b], axis=1), weight, (1, 0))


def left_kernel(n_a, *refs):
    a_refs, (*b_refs, q_ref, o_ref) = refs[:n_a], refs[n_a:]
    rows = o_ref.shape[0] // 2
    for first in (True, False):
        weight = pair_weight(q_ref, first)
        for start, stop in spans(a_refs, b_refs):
            to = 0 if first else rows
            o_ref[to + start : to + stop, :] = low(pair_dot(a_refs, b_refs, start, stop, weight, first))


def left_half(a, b, q):
    rows, cols = sum(v.shape[0] for v in a), a[0].shape[1]
    w = q.shape[1]
    return pl.pallas_call(
        functools.partial(left_kernel, len(a)),
        in_specs=whole(len(a) + len(b) + 1),
        out_specs=whole(1)[0],
        out_shape=jax.ShapeDtypeStruct((2 * rows, w), BF16),
        cost_estimate=pl.CostEstimate(flops=8 * rows * w * w, bytes_accessed=6 * rows * cols, transcendentals=0),
        compiler_params=params(),
        name="left_half",
    )(*a, *b, q)


def final_kernel(base, cuts, n_a, *refs):
    a_refs, (b_ref, l_ref, q_ref, *_, o_hbm, o_ref, sem) = refs[:n_a], refs[n_a:]
    rows, cols = l_ref.shape[0] // 2, o_ref.shape[1]
    copies = []
    for first in (True, False):
        weight = pair_weight(q_ref, first)
        for start, stop in cuts:
            a, b = span(a_refs, start, stop), b_ref.at[start - base : stop - base]
            right = pair_dot([a], [b], 0, stop - start, weight, first)
            to = slice(start, stop) if first else slice(rows + start, rows + stop)
            shift = -base if first else b_ref.shape[0] - base
            here = slice(start + shift, stop + shift)
            left = l_ref[to, :].astype(F32)
            packed_store(o_ref, here, left, right, cols // 2)
            copy = pltpu.make_async_copy(o_ref.at[here, :], o_hbm.at[to, :], sem.at[len(copies)])
            copy.start()
            copies.append(copy)
    for copy in copies:
        copy.wait()


def final(l, a, b, q):
    rows, cols = l.shape[0], a[0].shape[1]
    w = q.shape[1]
    out, base = [], 0
    for block in b:
        n = block.shape[0]
        cuts = [(i, j) for i, j in spans(a, b) if base <= i < base + n]
        args = (*a, block, l, q, *out)
        out = [
            pl.pallas_call(
                functools.partial(final_kernel, base, cuts, len(a)),
                in_specs=whole(len(a) + 3) + [pl.BlockSpec(memory_space=pltpu.HBM)] * len(out),
                out_specs=pl.BlockSpec(memory_space=pltpu.HBM),
                out_shape=jax.ShapeDtypeStruct((rows, cols), BF16),
                input_output_aliases={len(args) - 1: 0} if out else {},
                scratch_shapes=[pltpu.VMEM((2 * n, cols), BF16), pltpu.SemaphoreType.DMA((2 * len(cuts),))],
                cost_estimate=pl.CostEstimate(flops=8 * n * w * w, bytes_accessed=8 * n * cols, transcendentals=0),
                compiler_params=params(),
                name="final",
            )(*args)
        ]
        base += n
    return out[0]


def passed(x, by):
    n = lax.axis_size("pairs")
    return lax.ppermute(x, "pairs", [(i, (i + 2 * by) % n) for i in range(n)])


def row_parts(g):
    n = lax.axis_size("rows")
    if n & (n - 1) or n > 4:
        return [lax.psum(g.astype(F32), "rows")]
    return [g] + [lax.ppermute(g, "rows", [(i, i ^ k) for i in range(n)]) for k in range(1, n)]


def shares(rows, *parts):
    return [rows * e // 64 for e in parts]


def local(latent):
    rows = latent.shape[0] // 2
    head, middle, last = shares(rows, 34, 8, 22)
    raw_in = passed(taken(latent, last), 1)
    parts = row_parts(gram(latent, 4))
    s, share, a = rotor(parts, latent, [head, middle])
    share_in = passed(share, 1)
    a_in = [passed(a[0], 1)]
    a_in.append(passed(a[1], 1))
    b = rotate(s, latent, shares(rows, 44, 20))
    a.append(tail([s], latent, last))
    s_in = row_parts(share_in) if shared(latent.shape[1]) > 1 else [share_in]
    a_in.append(tail(s_in, raw_in, last))
    a_in[0], b_out = lax.optimization_barrier((a_in[0], b[0]))
    b_in = [passed(b_out, -1)]
    s, left = second(row_parts(gram_pair(a_in, b)))
    s_in = passed(s, -1)
    left, b_out = lax.optimization_barrier((left, b[1]))
    b_in.append(passed(b_out, -1))
    return final(left_half(a_in, b, left), a, b_in, right_of(s_in))


def solution(mesh):
    return jax.shard_map(
        local,
        mesh=mesh,
        in_specs=(P("rows", "pairs"),),
        out_specs=P("rows", "pairs"),
        check_vma=False,
    )
```

```python
import functools
import math

import jax
import jax.numpy as jnp
import numpy as np
from jax import lax
from jax.experimental import pallas as pl
from jax.experimental.pallas import tpu as pltpu
from jax.sharding import PartitionSpec as P


F32, BF16 = jnp.float32, jnp.bfloat16
LANES = 128


def polar_coefficients():
    c = 1.5 / math.sqrt(65.0)
    mul, sub = np.polynomial.polynomial.polymul, np.polynomial.polynomial.polysub
    n = np.array([c * c, c * c])
    u = np.array([1.5 - 0.5 * c * c, -0.5 * c * c])
    return [float(v) for v in c * sub(1.5 * u, 0.5 * mul(n, mul(u, mul(u, u))))]


COEF = polar_coefficients()


def window(half):
    return -(-half // LANES) * LANES


def dot(a, b, contract):
    return lax.dot_general(a, b, ((contract[:1], contract[1:]), ((), ())), preferred_element_type=F32)


def low(a):
    return a.astype(BF16)


def params():
    return pltpu.CompilerParams(vmem_limit_bytes=16 << 20)


def whole(n):
    return [pl.BlockSpec(memory_space=pltpu.VMEM)] * n


def pieces(rows, n):
    return [slice(i * (rows // n), (i + 1) * (rows // n)) for i in range(n)]


def spans(*lists):
    cuts = {0}
    for blocks in lists:
        stop = 0
        for block in blocks:
            stop += block.shape[0]
            cuts.add(stop)
    cuts = sorted(cuts)
    return list(zip(cuts[:-1], cuts[1:]))


def span(blocks, start, stop):
    for block in blocks:
        if start < block.shape[0]:
            return block.at[start:stop]
        start, stop = start - block.shape[0], stop - block.shape[0]


def blocks_of(cols, sizes):
    return [jax.ShapeDtypeStruct((n, cols), BF16) for n in sizes]


def pack_window(top, bot, half):
    w = top.shape[1]
    lane = lax.broadcasted_iota(jnp.int32, top.shape, 1)
    return jnp.where(lane < half, pltpu.roll(top, half, 1), 0.0), jnp.where(lane >= w - half, bot, 0.0)


def unpack_window(packed):
    cols = packed.shape[1]
    half = cols // 2
    w = window(half)
    return jnp.concatenate([pltpu.roll(packed[:, :w], w - half, 1), packed[:, cols - w :]], axis=0)


def pack_stats(g_ref, cross, norms):
    half, _ = cross.shape
    h = half // 2
    packed_store(g_ref, slice(0, h), *pack_window(cross[:h], cross[h:], half), half)
    row = lax.broadcasted_iota(jnp.int32, (8, g_ref.shape[1]), 0)
    rest = norms - low(norms).astype(F32)
    g_ref[h:] = low(jnp.where(row == 0, norms, jnp.where(row == 1, rest, 0.0)))


def stats_shape(cols):
    return jax.ShapeDtypeStruct((cols // 4 + 8, cols), BF16)


def taken_kernel(x_hbm, raw_ref, sem):
    rows, k = x_hbm.shape[0], raw_ref.shape[0] // 2
    copies = [
        pltpu.make_async_copy(x_hbm.at[stop - k : stop, :], raw_ref.at[i * k : (i + 1) * k, :], sem.at[i])
        for i, stop in enumerate((rows // 2, rows))
    ]
    for copy in copies:
        copy.start()
    for copy in copies:
        copy.wait()


def taken(x, k):
    cols = x.shape[1]
    return pl.pallas_call(
        taken_kernel,
        in_specs=[pl.BlockSpec(memory_space=pltpu.HBM)],
        out_specs=whole(1)[0],
        out_shape=jax.ShapeDtypeStruct((2 * k, cols), BF16),
        scratch_shapes=[pltpu.SemaphoreType.DMA((2,))],
        cost_estimate=pl.CostEstimate(flops=0, bytes_accessed=8 * k * cols, transcendentals=0),
        compiler_params=params(),
        name="taken",
    )(pltpu.with_memory_space_constraint(x, pltpu.HBM))


def gram_kernel(n, x_ref, g_ref):
    rows, cols = x_ref.shape
    half = cols // 2
    w = window(half)
    cross, norms = jnp.zeros((w, w), F32), jnp.zeros((1, cols), F32)
    for r in pieces(rows, n):
        x = x_ref[r, :]
        cross += dot(x[:, :w], x[:, cols - w :], (0, 0))
        xf = x.astype(F32)
        norms += jnp.sum(xf * xf, axis=0, keepdims=True)
    pack_stats(g_ref, cross[:half], norms)


def gram(x, n):
    rows, cols = x.shape
    w = window(cols // 2)
    return pl.pallas_call(
        functools.partial(gram_kernel, n),
        in_specs=whole(1),
        out_specs=whole(1)[0],
        out_shape=stats_shape(cols),
        cost_estimate=pl.CostEstimate(flops=2 * rows * w * w, bytes_accessed=2 * rows * cols, transcendentals=0),
        compiler_params=params(),
        name="gram",
    )(x)


def gram_pair_kernel(n_a, *refs):
    a_refs, b_refs, g_ref = refs[:n_a], refs[n_a:-1], refs[-1]
    cols = g_ref.shape[1]
    half = cols // 2
    w = window(half)
    pad, o = w - half, cols - w
    top, bot = jnp.zeros((w, w), F32), jnp.zeros((w, w), F32)
    norm_a, norm_b = jnp.zeros((1, cols), F32), jnp.zeros((1, cols), F32)
    for start, stop in spans(a_refs, b_refs):
        a, b = span(a_refs, start, stop)[...], span(b_refs, start, stop)[...]
        top += dot(a[:, :w], b[:, :w], (0, 0))
        bot += dot(a[:, o:], b[:, o:], (0, 0))
        af, bf = a.astype(F32), b.astype(F32)
        norm_a += jnp.sum(af * af, axis=0, keepdims=True)
        norm_b += jnp.sum(bf * bf, axis=0, keepdims=True)
    cross = pltpu.roll(top[:half], pad, 1) + bot[pad:]
    s, t = jnp.broadcast_to(norm_a, (8, cols)), jnp.broadcast_to(norm_b, (8, cols))
    left = s + jnp.concatenate([pltpu.roll(s[:, o:], half, 1), jnp.zeros((8, o), F32)], axis=1)
    right = t + jnp.concatenate([jnp.zeros((8, o), F32), pltpu.roll(t[:, :w], pad, 1)], axis=1)
    lane = lax.broadcasted_iota(jnp.int32, (8, cols), 1)
    pack_stats(g_ref, cross, jnp.where(lane < half, left, right)[:1])


def gram_pair(a, b):
    cols = a[0].shape[1]
    rows = sum(v.shape[0] for v in a)
    w = window(cols // 2)
    return pl.pallas_call(
        functools.partial(gram_pair_kernel, len(a)),
        in_specs=whole(len(a) + len(b)),
        out_specs=whole(1)[0],
        out_shape=stats_shape(cols),
        cost_estimate=pl.CostEstimate(flops=4 * rows * w * w, bytes_accessed=4 * rows * cols, transcendentals=0),
        compiler_params=params(),
        name="gram_pair",
    )(*a, *b)


def cross_of(parts):
    total = sum((p[...].astype(F32) for p in parts[1:]), parts[0][...].astype(F32))
    cols = total.shape[1]
    half = cols // 2
    w = window(half)
    pad, h = w - half, half // 2
    cross = unpack_window(total[:h])
    norms = total[h:] + pltpu.roll(total[h:], 7, 0)
    left = jnp.transpose(norms[:, :w])[:half, :1]
    corr = cross * (lax.rsqrt(left) * lax.rsqrt(norms[:1, cols - w :]))
    lane = lax.broadcasted_iota(jnp.int32, corr.shape, 1)
    corr = jnp.where(lane >= pad, corr, 0.0)
    size = jnp.sqrt(2.0 * jnp.sum(corr * corr) + 1e-12)
    return filled(corr * (8.0 / size))


def filled(x):
    half, w = x.shape
    return jnp.concatenate([x, jnp.zeros((w - half, w), F32)], axis=0) if w > half else x


def split(a):
    high = low(a)
    return high, low(a - high.astype(F32))


def split_dot(a, b, contract=(1, 0)):
    return dot(a[0], b[0], contract) + (dot(a[0], b[1], contract) + dot(a[1], b[0], contract))


def minus_constant(k):
    words = split(k)
    k2 = split_dot(words, words)
    return COEF[1] * k + COEF[2] * k2 + dot(low(k2), low(COEF[3] * k + COEF[4] * k2), (1, 0))


def word_dot(x, delta, contract):
    high, rest = split(delta)
    return dot(x, high, contract) + dot(x, rest, contract)


def eye_at(w, first, stop):
    r = lax.broadcasted_iota(jnp.int32, (w, w), 0)
    c = lax.broadcasted_iota(jnp.int32, (w, w), 1)
    return (r == c) & (r >= first) & (r < stop)


def left_columns(x, half):
    w = x.shape[1]
    xb = low(x)
    k = dot(xb, xb, (1, 1))
    delta = minus_constant(k)
    upper = delta + jnp.where(eye_at(w, 0, half), COEF[0], 0.0)
    lower = -(COEF[0] * jnp.transpose(x) + word_dot(xb, delta, (0, 0)))
    return low(jnp.concatenate([upper[:half], lower[w - half :]], axis=0))


def right_columns(x, half):
    w = x.shape[1]
    xb = low(x)
    k = dot(xb, xb, (0, 0))
    delta = minus_constant(k)
    upper = COEF[0] * x + word_dot(xb, delta, (1, 0))
    lower = delta + jnp.where(eye_at(w, w - half, w), COEF[0], 0.0)
    return low(jnp.concatenate([upper[:half], lower[w - half :]], axis=0))


def moved(q, by):
    return low(pltpu.roll(q.astype(F32), by, 1)) if by else q


def packed_store(ref, rows, top, bot, half):
    w = top.shape[1]
    o = 2 * half - w
    ref[rows, :o] = low(top[:, :o])
    if w > o:
        ref[rows, o:w] = low(top[:, o:] + bot[:, : w - o])
    ref[rows, w:] = low(bot[:, w - o :])


def rotate_into(refs, x_ref, q_top, q_bot, base=0):
    rows, half = x_ref.shape[0] // 2, x_ref.shape[1] // 2
    for start, stop in spans(refs):
        top = dot(x_ref[base + start : base + stop, :], q_top, (1, 0))
        bot = dot(x_ref[rows + base + start : rows + base + stop, :], q_bot, (1, 0))
        packed_store(span(refs, start, stop), slice(None), top, bot, half)


def rounded_factor(s_ref, s):
    h, cols = s_ref.shape
    packed_store(s_ref, slice(None), *pack_window(s[:h], s[h : 2 * h], cols // 2), cols // 2)


def own_share(s_ref, n):
    s = s_ref[...].astype(F32)
    h = s.shape[0] // n
    me, share = lax.axis_index("rows"), s[:h]
    for k in range(1, n):
        share = jnp.where(me == k, s[k * h : (k + 1) * h], share)
    return low(share)


def joined(share_refs):
    shares = [ref[...].astype(F32) for ref in share_refs]
    if len(shares) == 1:
        return shares[0]
    me, rows = lax.axis_index("rows"), []
    for at in range(len(shares)):
        row = shares[0]
        for k in range(1, len(shares)):
            row = jnp.where(me == at ^ k, shares[k], row)
        rows.append(row)
    return jnp.concatenate(rows, axis=0)


def shared(cols):
    n = lax.axis_size("rows")
    return n if n <= 4 and not n & (n - 1) and (cols // 4) % (8 * n) == 0 else 1


def factor(*share_refs):
    s = unpack_window(joined(share_refs))
    half, w = s.shape
    lane = lax.broadcasted_iota(jnp.int32, s.shape, 1)
    return filled(jnp.where(lane >= w - half, s, 0.0)), half


def left_pair(s, half):
    left = left_columns(s, half)
    return left, moved(left, s.shape[1] - half)


def rotor_kernel(n_parts, *refs):
    parts = refs[:n_parts]
    x_ref, s_ref, share_ref, *a_refs = refs[n_parts:]
    s = cross_of(parts)
    rounded_factor(s_ref, s)
    share_ref[...] = own_share(s_ref, s_ref.shape[0] // share_ref.shape[0])
    rotate_into(a_refs, x_ref, *left_pair(low(s).astype(F32), x_ref.shape[1] // 2))


def rotor(parts, x, sizes):
    _, cols = x.shape
    w = window(cols // 2)
    s, share, *a = pl.pallas_call(
        functools.partial(rotor_kernel, len(parts)),
        in_specs=whole(len(parts) + 1),
        out_specs=whole(2 + len(sizes)),
        out_shape=blocks_of(cols, [cols // 4, cols // 4 // shared(cols)] + sizes),
        cost_estimate=pl.CostEstimate(flops=4 * sum(sizes) * cols * w, bytes_accessed=6 * sum(sizes) * cols, transcendentals=0),
        compiler_params=params(),
        name="rotor",
    )(*parts, x)
    return s, share, a


def tail_kernel(*refs):
    *s_refs, x_ref, a_ref = refs
    rotate_into([a_ref], x_ref, *left_pair(*factor(*s_refs)), base=x_ref.shape[0] // 2 - a_ref.shape[0])


def tail(s, x, k):
    cols = x.shape[1]
    w = window(cols // 2)
    return pl.pallas_call(
        tail_kernel,
        in_specs=whole(len(s) + 1),
        out_specs=whole(1)[0],
        out_shape=jax.ShapeDtypeStruct((k, cols), BF16),
        cost_estimate=pl.CostEstimate(flops=4 * k * cols * w, bytes_accessed=6 * k * cols, transcendentals=0),
        compiler_params=params(),
        name="tail",
    )(*s, x)


def rotate_kernel(s_ref, x_ref, *b_refs):
    s, half = factor(s_ref)
    right = right_columns(s, half)
    rotate_into(b_refs, x_ref, moved(right, half), right)


def rotate(s, x, sizes):
    rows, cols = x.shape
    w = window(cols // 2)
    return pl.pallas_call(
        rotate_kernel,
        in_specs=whole(2),
        out_specs=whole(len(sizes)),
        out_shape=blocks_of(cols, sizes),
        cost_estimate=pl.CostEstimate(flops=2 * rows * cols * w, bytes_accessed=3 * rows * cols, transcendentals=0),
        compiler_params=params(),
        name="rotate",
    )(s, x)


def second_kernel(*refs):
    *parts, s_ref = refs
    rounded_factor(s_ref, cross_of(parts))


def second(parts):
    cols = parts[0].shape[1]
    w = window(cols // 2)
    return pl.pallas_call(
        second_kernel,
        in_specs=whole(len(parts)),
        out_specs=whole(1)[0],
        out_shape=jax.ShapeDtypeStruct((cols // 4, cols), BF16),
        cost_estimate=pl.CostEstimate(flops=8 * w**2, bytes_accessed=4 * w * w, transcendentals=0),
        compiler_params=params(),
        name="second",
    )(*parts)


def left_factor_kernel(s_ref, left_ref):
    left_ref[...] = left_columns(*factor(s_ref))


def columns_of(kernel, s):
    cols = s.shape[1]
    w = window(cols // 2)
    return pl.pallas_call(
        kernel,
        in_specs=whole(1),
        out_specs=whole(1)[0],
        out_shape=jax.ShapeDtypeStruct((cols, w), BF16),
        cost_estimate=pl.CostEstimate(flops=8 * w**3, bytes_accessed=4 * w * w, transcendentals=0),
        compiler_params=params(),
    )(s)


def pair_weight(q_ref, first):
    cols, w = q_ref.shape
    half = cols // 2
    rest = jnp.zeros((w - half, w), BF16)
    upper, lower = q_ref[:half], q_ref[half:]
    return jnp.concatenate([upper, rest, lower, rest] if first else [rest, upper, rest, lower], axis=0)


def pair_dot(a_refs, b_refs, start, stop, weight, first):
    w = weight.shape[1]
    cols = a_refs[0].shape[1]
    at = slice(0, w) if first else slice(cols - w, cols)
    a, b = span(a_refs, start, stop)[:, at], span(b_refs, start, stop)[:, at]
    return dot(jnp.concatenate([a, b], axis=1), weight, (1, 0))


def left_kernel(n_a, *refs):
    a_refs, (*b_refs, q_ref, o_ref) = refs[:n_a], refs[n_a:]
    rows = o_ref.shape[0] // 2
    for first in (True, False):
        weight = pair_weight(q_ref, first)
        for start, stop in spans(a_refs, b_refs):
            to = 0 if first else rows
            o_ref[to + start : to + stop, :] = low(pair_dot(a_refs, b_refs, start, stop, weight, first))


def left_half(a, b, q):
    rows, cols = sum(v.shape[0] for v in a), a[0].shape[1]
    w = q.shape[1]
    return pl.pallas_call(
        functools.partial(left_kernel, len(a)),
        in_specs=whole(len(a) + len(b) + 1),
        out_specs=whole(1)[0],
        out_shape=jax.ShapeDtypeStruct((2 * rows, w), BF16),
        cost_estimate=pl.CostEstimate(flops=8 * rows * w * w, bytes_accessed=6 * rows * cols, transcendentals=0),
        compiler_params=params(),
        name="left_half",
    )(*a, *b, q)


def final_kernel(base, cuts, n_a, *refs):
    a_refs, (b_ref, l_ref, q_ref, *_, o_ref, sem) = refs[:n_a], refs[n_a:]
    o_hbm = refs[n_a + 3] if base == 0 else refs[n_a + 4]
    if base == 0:
        refs[n_a + 4][...] = right_columns(*factor(q_ref))
        q_ref = refs[n_a + 4]
    rows, cols = l_ref.shape[0] // 2, o_ref.shape[1]
    copies = []
    for first in (True, False):
        weight = pair_weight(q_ref, first)
        for start, stop in cuts:
            a, b = span(a_refs, start, stop), b_ref.at[start - base : stop - base]
            right = pair_dot([a], [b], 0, stop - start, weight, first)
            to = slice(start, stop) if first else slice(rows + start, rows + stop)
            shift = -base if first else b_ref.shape[0] - base
            here = slice(start + shift, stop + shift)
            left = l_ref[to, :].astype(F32)
            packed_store(o_ref, here, left, right, cols // 2)
            copy = pltpu.make_async_copy(o_ref.at[here, :], o_hbm.at[to, :], sem.at[len(copies)])
            copy.start()
            copies.append(copy)
    for copy in copies:
        copy.wait()


def final(l, a, b, s):
    rows, cols, w = l.shape[0], a[0].shape[1], l.shape[1]
    result, weight, base = None, s, 0
    for block in b:
        n = block.shape[0]
        first = base == 0
        cuts = [(i, j) for i, j in spans(a, b) if base <= i < base + n]
        args = (*a, block, l, weight) + (() if first else (result,))
        result, *made = pl.pallas_call(
            functools.partial(final_kernel, base, cuts, len(a)),
            in_specs=whole(len(a) + 3) + ([] if first else [pl.BlockSpec(memory_space=pltpu.HBM)]),
            out_specs=[pl.BlockSpec(memory_space=pltpu.HBM)] + (whole(1) if first else []),
            out_shape=[jax.ShapeDtypeStruct((rows, cols), BF16)] + (blocks_of(w, [cols]) if first else []),
            input_output_aliases={} if first else {len(args) - 1: 0},
            scratch_shapes=[pltpu.VMEM((2 * n, cols), BF16), pltpu.SemaphoreType.DMA((2 * len(cuts),))],
            cost_estimate=pl.CostEstimate(flops=8 * n * w * w, bytes_accessed=8 * n * cols, transcendentals=0),
            compiler_params=params(),
            name="final",
        )(*args)
        weight = made[0] if first else weight
        base += n
    return result


def passed(x, by):
    n = lax.axis_size("pairs")
    return lax.ppermute(x, "pairs", [(i, (i + 2 * by) % n) for i in range(n)])


def row_parts(g):
    n = lax.axis_size("rows")
    if n & (n - 1) or n > 4:
        return [lax.psum(g.astype(F32), "rows")]
    return [g] + [lax.ppermute(g, "rows", [(i, i ^ k) for i in range(n)]) for k in range(1, n)]


def shares(rows, *parts):
    return [rows * e // 64 for e in parts]


def local(latent):
    rows = latent.shape[0] // 2
    head, middle, last = shares(rows, 34, 8, 22)
    raw_in = passed(taken(latent, last), 1)
    parts = row_parts(gram(latent, 4))
    s, share, a = rotor(parts, latent, [head, middle])
    share_in = passed(share, 1)
    a_in = [passed(a[0], 1)]
    a_in.append(passed(a[1], 1))
    b = rotate(s, latent, shares(rows, 42, 22))
    a.append(tail([s], latent, last))
    s_in = row_parts(share_in) if shared(latent.shape[1]) > 1 else [share_in]
    a_in.append(tail(s_in, raw_in, last))
    a_in[0], b_out = lax.optimization_barrier((a_in[0], b[0]))
    b_in = [passed(b_out, -1)]
    stats = gram_pair(a_in, b)
    parts = row_parts(stats)
    s = second(parts)
    s_in = passed(s, -1)
    s, *rest = lax.optimization_barrier((s, *b[1:]))
    for block in rest:
        b_in.append(passed(block, -1))
    left = columns_of(left_factor_kernel, s)
    return final(left_half(a_in, b, left), a, b_in, s_in)


def solution(mesh):
    return jax.shard_map(
        local,
        mesh=mesh,
        in_specs=(P("rows", "pairs"),),
        out_specs=P("rows", "pairs"),
        check_vma=False,
    )
```

```python
import functools
import math

import jax
import jax.numpy as jnp
import numpy as np
from jax import lax
from jax.experimental import pallas as pl
from jax.experimental.pallas import tpu as pltpu
from jax.sharding import PartitionSpec as P


F32, BF16 = jnp.float32, jnp.bfloat16
LANES = 128


def polar_coefficients():
    c = 1.5 / math.sqrt(65.0)
    mul, sub = np.polynomial.polynomial.polymul, np.polynomial.polynomial.polysub
    n = np.array([c * c, c * c])
    u = np.array([1.5 - 0.5 * c * c, -0.5 * c * c])
    return [float(v) for v in c * sub(1.5 * u, 0.5 * mul(n, mul(u, mul(u, u))))]


COEF = polar_coefficients()


def window(half):
    return -(-half // LANES) * LANES


def dot(a, b, contract):
    return lax.dot_general(a, b, ((contract[:1], contract[1:]), ((), ())), preferred_element_type=F32)


def low(a):
    return a.astype(BF16)


def params():
    return pltpu.CompilerParams(vmem_limit_bytes=16 << 20)


def whole(n):
    return [pl.BlockSpec(memory_space=pltpu.VMEM)] * n


def pieces(rows, n):
    return [slice(i * (rows // n), (i + 1) * (rows // n)) for i in range(n)]


def spans(*lists):
    cuts = {0}
    for blocks in lists:
        stop = 0
        for block in blocks:
            stop += block.shape[0]
            cuts.add(stop)
    cuts = sorted(cuts)
    return list(zip(cuts[:-1], cuts[1:]))


def span(blocks, start, stop):
    for block in blocks:
        if start < block.shape[0]:
            return block.at[start:stop]
        start, stop = start - block.shape[0], stop - block.shape[0]


def blocks_of(cols, sizes):
    return [jax.ShapeDtypeStruct((n, cols), BF16) for n in sizes]


def pack_window(top, bot, half):
    w = top.shape[1]
    lane = lax.broadcasted_iota(jnp.int32, top.shape, 1)
    return jnp.where(lane < half, pltpu.roll(top, half, 1), 0.0), jnp.where(lane >= w - half, bot, 0.0)


def unpack_window(packed):
    cols = packed.shape[1]
    half = cols // 2
    w = window(half)
    return jnp.concatenate([pltpu.roll(packed[:, :w], w - half, 1), packed[:, cols - w :]], axis=0)


def pack_stats(g_ref, cross, norms):
    half, _ = cross.shape
    h = half // 2
    packed_store(g_ref, slice(0, h), *pack_window(cross[:h], cross[h:], half), half)
    row = lax.broadcasted_iota(jnp.int32, (8, g_ref.shape[1]), 0)
    rest = norms - low(norms).astype(F32)
    g_ref[h:] = low(jnp.where(row == 0, norms, jnp.where(row == 1, rest, 0.0)))


def stats_shape(cols):
    return jax.ShapeDtypeStruct((cols // 4 + 8, cols), BF16)


def taken_kernel(x_hbm, raw_ref, sem):
    rows, k = x_hbm.shape[0], raw_ref.shape[0] // 2
    copies = [
        pltpu.make_async_copy(x_hbm.at[stop - k : stop, :], raw_ref.at[i * k : (i + 1) * k, :], sem.at[i])
        for i, stop in enumerate((rows // 2, rows))
    ]
    for copy in copies:
        copy.start()
    for copy in copies:
        copy.wait()


def taken(x, k):
    cols = x.shape[1]
    return pl.pallas_call(
        taken_kernel,
        in_specs=[pl.BlockSpec(memory_space=pltpu.HBM)],
        out_specs=whole(1)[0],
        out_shape=jax.ShapeDtypeStruct((2 * k, cols), BF16),
        scratch_shapes=[pltpu.SemaphoreType.DMA((2,))],
        cost_estimate=pl.CostEstimate(flops=0, bytes_accessed=8 * k * cols, transcendentals=0),
        compiler_params=params(),
        name="taken",
    )(pltpu.with_memory_space_constraint(x, pltpu.HBM))


def gram_kernel(n, x_ref, g_ref):
    rows, cols = x_ref.shape
    half = cols // 2
    w = window(half)
    cross, norms = jnp.zeros((w, w), F32), jnp.zeros((1, cols), F32)
    for r in pieces(rows, n):
        x = x_ref[r, :]
        cross += dot(x[:, :w], x[:, cols - w :], (0, 0))
        xf = x.astype(F32)
        norms += jnp.sum(xf * xf, axis=0, keepdims=True)
    pack_stats(g_ref, cross[:half], norms)


def gram(x, n):
    rows, cols = x.shape
    w = window(cols // 2)
    return pl.pallas_call(
        functools.partial(gram_kernel, n),
        in_specs=whole(1),
        out_specs=whole(1)[0],
        out_shape=stats_shape(cols),
        cost_estimate=pl.CostEstimate(flops=2 * rows * w * w, bytes_accessed=2 * rows * cols, transcendentals=0),
        compiler_params=params(),
        name="gram",
    )(x)


def gram_pair_kernel(n_a, *refs):
    a_refs, b_refs, g_ref = refs[:n_a], refs[n_a:-1], refs[-1]
    cols = g_ref.shape[1]
    half = cols // 2
    w = window(half)
    pad, o = w - half, cols - w
    top, bot = jnp.zeros((w, w), F32), jnp.zeros((w, w), F32)
    norm_a, norm_b = jnp.zeros((1, cols), F32), jnp.zeros((1, cols), F32)
    for start, stop in spans(a_refs, b_refs):
        a, b = span(a_refs, start, stop)[...], span(b_refs, start, stop)[...]
        top += dot(a[:, :w], b[:, :w], (0, 0))
        bot += dot(a[:, o:], b[:, o:], (0, 0))
        af, bf = a.astype(F32), b.astype(F32)
        norm_a += jnp.sum(af * af, axis=0, keepdims=True)
        norm_b += jnp.sum(bf * bf, axis=0, keepdims=True)
    cross = pltpu.roll(top[:half], pad, 1) + bot[pad:]
    s, t = jnp.broadcast_to(norm_a, (8, cols)), jnp.broadcast_to(norm_b, (8, cols))
    left = s + jnp.concatenate([pltpu.roll(s[:, o:], half, 1), jnp.zeros((8, o), F32)], axis=1)
    right = t + jnp.concatenate([jnp.zeros((8, o), F32), pltpu.roll(t[:, :w], pad, 1)], axis=1)
    lane = lax.broadcasted_iota(jnp.int32, (8, cols), 1)
    pack_stats(g_ref, cross, jnp.where(lane < half, left, right)[:1])


def gram_pair(a, b):
    cols = a[0].shape[1]
    rows = sum(v.shape[0] for v in a)
    w = window(cols // 2)
    return pl.pallas_call(
        functools.partial(gram_pair_kernel, len(a)),
        in_specs=whole(len(a) + len(b)),
        out_specs=whole(1)[0],
        out_shape=stats_shape(cols),
        cost_estimate=pl.CostEstimate(flops=4 * rows * w * w, bytes_accessed=4 * rows * cols, transcendentals=0),
        compiler_params=params(),
        name="gram_pair",
    )(*a, *b)


def cross_of(parts):
    total = sum((p[...].astype(F32) for p in parts[1:]), parts[0][...].astype(F32))
    cols = total.shape[1]
    half = cols // 2
    w = window(half)
    pad, h = w - half, half // 2
    cross = unpack_window(total[:h])
    norms = total[h:] + pltpu.roll(total[h:], 7, 0)
    left = jnp.transpose(norms[:, :w])[:half, :1]
    corr = cross * (lax.rsqrt(left) * lax.rsqrt(norms[:1, cols - w :]))
    lane = lax.broadcasted_iota(jnp.int32, corr.shape, 1)
    corr = jnp.where(lane >= pad, corr, 0.0)
    size = jnp.sqrt(2.0 * jnp.sum(corr * corr) + 1e-12)
    return filled(corr * (8.0 / size))


def filled(x):
    half, w = x.shape
    return jnp.concatenate([x, jnp.zeros((w - half, w), F32)], axis=0) if w > half else x


def split(a):
    high = low(a)
    return high, low(a - high.astype(F32))


def split_dot(a, b, contract=(1, 0)):
    return dot(a[0], b[0], contract) + (dot(a[0], b[1], contract) + dot(a[1], b[0], contract))


def minus_constant(k):
    words = split(k)
    k2 = split_dot(words, words)
    return COEF[1] * k + COEF[2] * k2 + dot(low(k2), low(COEF[3] * k + COEF[4] * k2), (1, 0))


def word_dot(x, delta, contract):
    high, rest = split(delta)
    return dot(x, high, contract) + dot(x, rest, contract)


def eye_at(w, first, stop):
    r = lax.broadcasted_iota(jnp.int32, (w, w), 0)
    c = lax.broadcasted_iota(jnp.int32, (w, w), 1)
    return (r == c) & (r >= first) & (r < stop)


def left_columns(x, half):
    w = x.shape[1]
    xb = low(x)
    k = dot(xb, xb, (1, 1))
    delta = minus_constant(k)
    upper = delta + jnp.where(eye_at(w, 0, half), COEF[0], 0.0)
    lower = -(COEF[0] * jnp.transpose(x) + word_dot(xb, delta, (0, 0)))
    return low(jnp.concatenate([upper[:half], lower[w - half :]], axis=0))


def right_columns(x, half):
    w = x.shape[1]
    xb = low(x)
    k = dot(xb, xb, (0, 0))
    delta = minus_constant(k)
    upper = COEF[0] * x + word_dot(xb, delta, (1, 0))
    lower = delta + jnp.where(eye_at(w, w - half, w), COEF[0], 0.0)
    return low(jnp.concatenate([upper[:half], lower[w - half :]], axis=0))


def moved(q, by):
    return low(pltpu.roll(q.astype(F32), by, 1)) if by else q


def packed_store(ref, rows, top, bot, half):
    w = top.shape[1]
    o = 2 * half - w
    ref[rows, :o] = low(top[:, :o])
    if w > o:
        ref[rows, o:w] = low(top[:, o:] + bot[:, : w - o])
    ref[rows, w:] = low(bot[:, w - o :])


def rotate_into(refs, x_ref, q_top, q_bot, base=0):
    rows, half = x_ref.shape[0] // 2, x_ref.shape[1] // 2
    for start, stop in spans(refs):
        top = dot(x_ref[base + start : base + stop, :], q_top, (1, 0))
        bot = dot(x_ref[rows + base + start : rows + base + stop, :], q_bot, (1, 0))
        packed_store(span(refs, start, stop), slice(None), top, bot, half)


def rounded_factor(s_ref, s):
    h, cols = s_ref.shape
    packed_store(s_ref, slice(None), *pack_window(s[:h], s[h : 2 * h], cols // 2), cols // 2)


def own_share(s_ref, n):
    s = s_ref[...].astype(F32)
    h = s.shape[0] // n
    me, share = lax.axis_index("rows"), s[:h]
    for k in range(1, n):
        share = jnp.where(me == k, s[k * h : (k + 1) * h], share)
    return low(share)


def joined(share_refs):
    shares = [ref[...].astype(F32) for ref in share_refs]
    if len(shares) == 1:
        return shares[0]
    me, rows = lax.axis_index("rows"), []
    for at in range(len(shares)):
        row = shares[0]
        for k in range(1, len(shares)):
            row = jnp.where(me == at ^ k, shares[k], row)
        rows.append(row)
    return jnp.concatenate(rows, axis=0)


def shared(cols):
    n = lax.axis_size("rows")
    return n if n <= 4 and not n & (n - 1) and (cols // 4) % (8 * n) == 0 else 1


def factor(*share_refs):
    s = unpack_window(joined(share_refs))
    half, w = s.shape
    lane = lax.broadcasted_iota(jnp.int32, s.shape, 1)
    return filled(jnp.where(lane >= w - half, s, 0.0)), half


def left_pair(s, half):
    left = left_columns(s, half)
    return left, moved(left, s.shape[1] - half)


def rotor_kernel(n_parts, *refs):
    parts = refs[:n_parts]
    x_ref, s_ref, share_ref, *a_refs = refs[n_parts:]
    s = cross_of(parts)
    rounded_factor(s_ref, s)
    share_ref[...] = own_share(s_ref, s_ref.shape[0] // share_ref.shape[0])
    rotate_into(a_refs, x_ref, *left_pair(low(s).astype(F32), x_ref.shape[1] // 2))


def rotor(parts, x, sizes):
    _, cols = x.shape
    w = window(cols // 2)
    s, share, *a = pl.pallas_call(
        functools.partial(rotor_kernel, len(parts)),
        in_specs=whole(len(parts) + 1),
        out_specs=whole(2 + len(sizes)),
        out_shape=blocks_of(cols, [cols // 4, cols // 4 // shared(cols)] + sizes),
        cost_estimate=pl.CostEstimate(flops=4 * sum(sizes) * cols * w, bytes_accessed=6 * sum(sizes) * cols, transcendentals=0),
        compiler_params=params(),
        name="rotor",
    )(*parts, x)
    return s, share, a


def tail_kernel(*refs):
    *s_refs, x_ref, a_ref = refs
    rotate_into([a_ref], x_ref, *left_pair(*factor(*s_refs)), base=x_ref.shape[0] // 2 - a_ref.shape[0])


def tail(s, x, k):
    cols = x.shape[1]
    w = window(cols // 2)
    return pl.pallas_call(
        tail_kernel,
        in_specs=whole(len(s) + 1),
        out_specs=whole(1)[0],
        out_shape=jax.ShapeDtypeStruct((k, cols), BF16),
        cost_estimate=pl.CostEstimate(flops=4 * k * cols * w, bytes_accessed=6 * k * cols, transcendentals=0),
        compiler_params=params(),
        name="tail",
    )(*s, x)


def rotate_kernel(s_ref, x_ref, *b_refs):
    s, half = factor(s_ref)
    right = right_columns(s, half)
    rotate_into(b_refs, x_ref, moved(right, half), right)


def rotate(s, x, sizes):
    rows, cols = x.shape
    w = window(cols // 2)
    return pl.pallas_call(
        rotate_kernel,
        in_specs=whole(2),
        out_specs=whole(len(sizes)),
        out_shape=blocks_of(cols, sizes),
        cost_estimate=pl.CostEstimate(flops=2 * rows * cols * w, bytes_accessed=3 * rows * cols, transcendentals=0),
        compiler_params=params(),
        name="rotate",
    )(s, x)


def second_kernel(*refs):
    *parts, s_ref = refs
    rounded_factor(s_ref, cross_of(parts))


def second(parts):
    cols = parts[0].shape[1]
    w = window(cols // 2)
    return pl.pallas_call(
        second_kernel,
        in_specs=whole(len(parts)),
        out_specs=whole(1)[0],
        out_shape=jax.ShapeDtypeStruct((cols // 4, cols), BF16),
        cost_estimate=pl.CostEstimate(flops=8 * w**2, bytes_accessed=4 * w * w, transcendentals=0),
        compiler_params=params(),
        name="second",
    )(*parts)


def left_factor_kernel(s_ref, left_ref):
    left_ref[...] = left_columns(*factor(s_ref))


def columns_of(kernel, s):
    cols = s.shape[1]
    w = window(cols // 2)
    return pl.pallas_call(
        kernel,
        in_specs=whole(1),
        out_specs=whole(1)[0],
        out_shape=jax.ShapeDtypeStruct((cols, w), BF16),
        cost_estimate=pl.CostEstimate(flops=8 * w**3, bytes_accessed=4 * w * w, transcendentals=0),
        compiler_params=params(),
    )(s)


def pair_weight(q_ref, first):
    cols, w = q_ref.shape
    half = cols // 2
    rest = jnp.zeros((w - half, w), BF16)
    upper, lower = q_ref[:half], q_ref[half:]
    return jnp.concatenate([upper, rest, lower, rest] if first else [rest, upper, rest, lower], axis=0)


def pair_dot(a_refs, b_refs, start, stop, weight, first):
    w = weight.shape[1]
    cols = a_refs[0].shape[1]
    at = slice(0, w) if first else slice(cols - w, cols)
    a, b = span(a_refs, start, stop)[:, at], span(b_refs, start, stop)[:, at]
    return dot(jnp.concatenate([a, b], axis=1), weight, (1, 0))


def left_kernel(n_a, *refs):
    a_refs, (*b_refs, q_ref, o_ref) = refs[:n_a], refs[n_a:]
    rows = o_ref.shape[0] // 2
    for first in (True, False):
        weight = pair_weight(q_ref, first)
        for start, stop in spans(a_refs, b_refs):
            to = 0 if first else rows
            o_ref[to + start : to + stop, :] = low(pair_dot(a_refs, b_refs, start, stop, weight, first))


def left_half(a, b, q):
    rows, cols = sum(v.shape[0] for v in a), a[0].shape[1]
    w = q.shape[1]
    return pl.pallas_call(
        functools.partial(left_kernel, len(a)),
        in_specs=whole(len(a) + len(b) + 1),
        out_specs=whole(1)[0],
        out_shape=jax.ShapeDtypeStruct((2 * rows, w), BF16),
        cost_estimate=pl.CostEstimate(flops=8 * rows * w * w, bytes_accessed=6 * rows * cols, transcendentals=0),
        compiler_params=params(),
        name="left_half",
    )(*a, *b, q)


def final_kernel(base, cuts, n_a, *refs):
    a_refs, (b_ref, l_ref, q_ref, *_, o_ref, sem) = refs[:n_a], refs[n_a:]
    o_hbm = refs[n_a + 3] if base == 0 else refs[n_a + 4]
    if base == 0:
        refs[n_a + 4][...] = right_columns(*factor(q_ref))
        q_ref = refs[n_a + 4]
    rows, cols = l_ref.shape[0] // 2, o_ref.shape[1]
    copies = []
    for first in (True, False):
        weight = pair_weight(q_ref, first)
        for start, stop in cuts:
            a, b = span(a_refs, start, stop), b_ref.at[start - base : stop - base]
            right = pair_dot([a], [b], 0, stop - start, weight, first)
            to = slice(start, stop) if first else slice(rows + start, rows + stop)
            shift = -base if first else b_ref.shape[0] - base
            here = slice(start + shift, stop + shift)
            left = l_ref[to, :].astype(F32)
            packed_store(o_ref, here, left, right, cols // 2)
            copy = pltpu.make_async_copy(o_ref.at[here, :], o_hbm.at[to, :], sem.at[len(copies)])
            copy.start()
            copies.append(copy)
    for copy in copies:
        copy.wait()


def final(l, a, b, s):
    rows, cols, w = l.shape[0], a[0].shape[1], l.shape[1]
    result, weight, base = None, s, 0
    for block in b:
        n = block.shape[0]
        first = base == 0
        cuts = []
        for i, j in spans(a, b):
            if base <= i < base + n:
                middle = (i + j) // 2 if (j - i) % 32 == 0 else j
                cuts += [(i, middle), (middle, j)] if middle < j else [(i, j)]
        args = (*a, block, l, weight) + (() if first else (result,))
        result, *made = pl.pallas_call(
            functools.partial(final_kernel, base, cuts, len(a)),
            in_specs=whole(len(a) + 3) + ([] if first else [pl.BlockSpec(memory_space=pltpu.HBM)]),
            out_specs=[pl.BlockSpec(memory_space=pltpu.HBM)] + (whole(1) if first else []),
            out_shape=[jax.ShapeDtypeStruct((rows, cols), BF16)] + (blocks_of(w, [cols]) if first else []),
            input_output_aliases={} if first else {len(args) - 1: 0},
            scratch_shapes=[pltpu.VMEM((2 * n, cols), BF16), pltpu.SemaphoreType.DMA((2 * len(cuts),))],
            cost_estimate=pl.CostEstimate(flops=8 * n * w * w, bytes_accessed=8 * n * cols, transcendentals=0),
            compiler_params=params(),
            name="final",
        )(*args)
        weight = made[0] if first else weight
        base += n
    return result


def passed(x, by):
    n = lax.axis_size("pairs")
    return lax.ppermute(x, "pairs", [(i, (i + 2 * by) % n) for i in range(n)])


def row_parts(g):
    n = lax.axis_size("rows")
    if n & (n - 1) or n > 4:
        return [lax.psum(g.astype(F32), "rows")]
    return [g] + [lax.ppermute(g, "rows", [(i, i ^ k) for i in range(n)]) for k in range(1, n)]


def shares(rows, *parts):
    return [rows * e // 64 for e in parts]


def local(latent):
    rows = latent.shape[0] // 2
    head, middle, last = shares(rows, 34, 8, 22)
    raw_in = passed(taken(latent, last), 1)
    parts = row_parts(gram(latent, 4))
    s, share, a = rotor(parts, latent, [head, middle])
    share_in = passed(share, 1)
    a_in = [passed(a[0], 1)]
    a_in.append(passed(a[1], 1))
    b = rotate(s, latent, shares(rows, 42, 22))
    a.append(tail([s], latent, last))
    s_in = row_parts(share_in) if shared(latent.shape[1]) > 1 else [share_in]
    a_in.append(tail(s_in, raw_in, last))
    a_in[0], b_out = lax.optimization_barrier((a_in[0], b[0]))
    b_in = [passed(b_out, -1)]
    stats = gram_pair(a_in, b)
    parts = row_parts(stats)
    s = second(parts)
    s_in = passed(s, -1)
    s, *rest = lax.optimization_barrier((s, *b[1:]))
    for block in rest:
        b_in.append(passed(block, -1))
    left = columns_of(left_factor_kernel, s)
    return final(left_half(a_in, b, left), a, b_in, s_in)


def solution(mesh):
    return jax.shard_map(
        local,
        mesh=mesh,
        in_specs=(P("rows", "pairs"),),
        out_specs=P("rows", "pairs"),
        check_vma=False,
    )
```
